256 devices in a mesh: tm: 8 (over z), paths: 32 (over y, x, core).
Axes of the slice: x: 4, y: 4, z: 8, core: 2. Of those that a mesh axis runs over, the one named last changes fastest.
Arguments:
- start_curve: float32 [80], replicated, may hold values from 0.02 to 0.06
- loadings: float32 [4, 80], replicated, may hold values from 0.2 to 1
- vols: float32 [40, 80], P('tm'), may hold values from 0.08 to 0.4
- shocks: float32 [40, 4, 65536], P('tm', None, 'paths'), may hold values from -5 to 5
- exercise_bits: int32 [40, 65536], P('tm', 'paths'), may hold values 0 or 1
- regress: float32 [40, 6], P('tm'), may hold values from -0.03 to 0.03
- date_slot: int32 [40], P('tm'), may hold values from 0 to 39, each once
- ck_rates: float32 [8, 80, 65536], P('tm', None, 'paths'), may hold values from 0.02 to 0.07
- ck_numer: float32 [8, 65536], P('tm', 'paths'), may hold values from 1 to 3
- ck_survive: float32 [8, 65536], P('tm', 'paths'), may hold values from 0.2 to 1
Outputs:
- vega: float32 [40, 80], P('tm')
- path_value: float32 [65536], P('paths')
The draws below stay inside these ranges and needn't reach their ends.
Inputs may be any that keep to these rules, and one draw needn't show every extreme that they name: `date_slot`: each row of regress is named once: a permutation of the 40 rows.
All inputs are finite; a program needn't handle non-finite values. No bound on the sum of `exercise_bits` on one device may be relied on, other than what follows from the above.
Results may differ from the reference program's by a relative error of at most 0.0003.
Values sent between devices are 32-bit elements; how exact they have to be, the bound alone decides.
A program may use at most 128 MiB of HBM per device.

```python
import math
import jax
import jax.numpy as jnp
from jax import lax

NF = 80
NE = 40
FACTORS = 4
BASIS = 6
PATHS = 65536
SHARDS = 8
N_TM = 8
N_PATHS = 32


def plant(result, key, low, top_value):
    dims = result.shape
    place = [jax.random.randint(jax.random.fold_in(key, axis), (), 0, dims[axis]) for axis in range(len(dims))]
    result = result.at[tuple(place)].set(low)
    longest = dims.index(max(dims))
    place[longest] = (place[longest] + 1) % dims[longest]
    return result.at[tuple(place)].set(top_value)


def block_scale(key, extent, split, smallest, high):
    def one(axis_at, parts):
        heights = jax.random.uniform(jax.random.fold_in(jax.random.fold_in(key, 6), axis_at), (parts,), jnp.float32, smallest / len(split), high / len(split))
        return jnp.repeat(jnp.exp(heights), extent[axis_at] // parts).reshape((-1,) + (1,) * (len(extent) - axis_at - 1))

    factor_of = one(*split[0])
    for cut in split[1:]:
        factor_of = factor_of * one(*cut)
    return factor_of


def bell_draw(rng, extent, deviation, most, pieces=(), kind=jnp.bfloat16):
    drawn = jax.random.normal(rng, extent, jnp.float32) * deviation
    if len(pieces) > 0:
        drawn = block_scale(rng, extent, pieces, -0.22, 0.18) * drawn
    return jnp.clip(drawn, min=-most, max=most).astype(kind)


def setup_inputs(seed: int = 0) -> dict:
    splits = jax.random.split(jax.random.key(seed), 11)
    start_curve = jnp.clip(jax.random.uniform(splits[0], (NF,), jnp.float32, 0.02, 0.06), 0.02, 0.06)
    loadings = jnp.clip(jax.random.uniform(splits[1], (FACTORS, NF), jnp.float32, 0.2, 1.0), 0.2, 1.0)
    vols = jnp.clip(jnp.exp(math.log(0.4) - 1.609438 * jax.random.uniform(splits[2], (NE, NF), jnp.float32) ** block_scale(splits[2], (NE, NF), ((0, 8),), -0.2, 0.2)), 0.08, 0.4)
    shocks = bell_draw(splits[3], (NE, FACTORS, PATHS), 1.0, 5.0, ((0, 8), (2, 32)), jnp.float32)
    exercise_bits = plant((jax.random.randint(splits[4], (NE, PATHS), 0, 2) < 1).astype(jnp.int32), jax.random.fold_in(splits[4], 1), 0, 1)
    regress = bell_draw(splits[5], (NE, BASIS), 0.005, 0.03, ((0, 8),), jnp.float32)
    date_slot = jax.random.permutation(splits[6], NE).astype(jnp.int32)
    ck_rates = jnp.clip(0.02 + 0.05 * jax.random.uniform(splits[7], (SHARDS, NF, PATHS), jnp.float32) ** block_scale(splits[7], (SHARDS, NF, PATHS), ((0, 8), (2, 32)), -0.2, 0.2), 0.02, 0.07)
    ck_numer = jnp.clip(1.0 + 2.0 * jax.random.uniform(splits[8], (SHARDS, PATHS), jnp.float32) ** block_scale(splits[8], (SHARDS, PATHS), ((0, 8), (1, 32)), -0.2, 0.2), 1.0, 3.0)
    ck_survive = jnp.clip(0.2 + 0.8 * jax.random.uniform(splits[9], (SHARDS, PATHS), jnp.float32) ** block_scale(splits[9], (SHARDS, PATHS), ((0, 8), (1, 32)), -0.2, 0.2), 0.2, 1.0)
    return dict(start_curve=start_curve, loadings=loadings, vols=vols, shocks=shocks, exercise_bits=exercise_bits, regress=regress, date_slot=date_slot, ck_rates=ck_rates, ck_numer=ck_numer, ck_survive=ck_survive)


ACCRUAL = 0.25
STRIKE = 0.04
SMOOTHING = 0.01
NOTIONAL = 100.0
HIGHEST = lax.Precision.HIGHEST

def segment(rates_in, numeraire, survival, vol_rows, shock_rows, flag_rows, weight_rows, loadings, first_date):
    forwards = rates_in.shape[0]
    positions = jnp.arange(forwards, dtype=jnp.int32)
    triangle = (positions[:, None] >= positions[None, :]).astype(jnp.float32)
    factor_loads = loadings / jnp.sqrt(lax.optimization_barrier(jnp.sum(loadings * loadings, axis=0, keepdims=True)))
    current = rates_in
    path_total = jnp.zeros(numeraire.shape, jnp.float32)
    for offset_date in range(vol_rows.shape[0]):
        date_index = first_date + offset_date
        opening = 2 * date_index + 1
        earlier = jnp.where(date_index == 0, 0, 2 * date_index - 1)
        horizon = jnp.where(date_index == 0, ACCRUAL, 2.0 * ACCRUAL)
        growth = jnp.log1p(ACCRUAL * current)
        fixing = ((positions >= earlier) & (positions < opening)).astype(jnp.float32)
        numeraire = numeraire * jnp.exp(lax.optimization_barrier(jnp.sum(fixing[:, None] * growth, axis=0)))
        living = (positions >= opening).astype(jnp.float32)
        sigma = vol_rows[offset_date] * living
        scaled = ACCRUAL * current * sigma[:, None] / (1.0 + ACCRUAL * current)
        running = jnp.einsum('ij,fjp->fip', triangle, factor_loads[:, :, None] * scaled[None], precision=HIGHEST)
        drift = sigma[:, None] * lax.optimization_barrier(jnp.sum(factor_loads[:, :, None] * running, axis=0))
        noise = jnp.einsum('fi,fp->ip', factor_loads, shock_rows[offset_date], precision=HIGHEST)
        exponent = horizon * drift - 0.5 * horizon * (sigma * sigma)[:, None] + jnp.sqrt(horizon) * sigma[:, None] * noise
        current = current * jnp.exp(exponent)
        discount = jnp.dot(triangle, living[:, None] * jnp.log1p(ACCRUAL * current), precision=HIGHEST)
        bonds = jnp.exp(-discount)
        annuity = ACCRUAL * lax.optimization_barrier(jnp.sum(living[:, None] * bonds, axis=0))
        floating = 1.0 - bonds[forwards - 1]
        exercise = floating - STRIKE * annuity
        moneyness = (floating / annuity - STRIKE) / SMOOTHING
        basis = jnp.stack([jnp.ones_like(moneyness), moneyness, moneyness * moneyness, annuity, annuity * moneyness, annuity * moneyness * moneyness])
        continuation = jnp.einsum('b,bp->p', weight_rows[offset_date], basis, precision=HIGHEST)
        chance = flag_rows[offset_date] * jax.nn.sigmoid((exercise - continuation) / SMOOTHING)
        path_total = path_total + NOTIONAL * survival * chance * exercise / numeraire
        survival = survival * (1.0 - chance)
    return (current, numeraire, survival, path_total)

def chained(every_vols, every_weights, shock_block, flag_block, rate_block, numer_block, survive_block, start_curve, loadings, per_shard, shard_count):
    width_paths = shock_block.shape[2]
    current = jnp.broadcast_to(start_curve[:, None], (start_curve.shape[0], width_paths))
    numeraire = jnp.ones((width_paths,), jnp.float32)
    survival = jnp.ones((width_paths,), jnp.float32)
    running_total = jnp.zeros((width_paths,), jnp.float32)
    for shard_index in range(shard_count):
        if shard_index > 0:
            current = rate_block[shard_index - 1] + (current - lax.stop_gradient(current))
            numeraire = numer_block[shard_index - 1] + (numeraire - lax.stop_gradient(numeraire))
            survival = survive_block[shard_index - 1] + (survival - lax.stop_gradient(survival))
        first_row = shard_index * per_shard
        last_row = first_row + per_shard
        current, numeraire, survival, segment_value = segment(current, numeraire, survival, every_vols[first_row:last_row], shock_block[first_row:last_row], flag_block[first_row:last_row], every_weights[first_row:last_row], loadings, first_row)
        running_total = running_total + segment_value
    return running_total

def reference(start_curve, loadings, vols, shocks, exercise_bits, regress, date_slot, ck_rates, ck_numer, ck_survive):
    per_shard = NE // N_TM
    per_group = PATHS // N_PATHS
    date_weights = regress[date_slot]
    flag_rows = exercise_bits.astype(jnp.float32)

    def one_group(vega_total, group_index):
        first_path = (group_index * per_group).astype(jnp.int32)

        def cut_paths(array_in, axis_number):
            return lax.dynamic_slice_in_dim(array_in, first_path, per_group, axis_number)
        shock_block = cut_paths(shocks, 2)
        flag_block = cut_paths(flag_rows, 1)
        rate_block = cut_paths(ck_rates, 2)
        numer_block = cut_paths(ck_numer, 1)
        survive_block = cut_paths(ck_survive, 1)

        def runner(every_vols):
            return chained(every_vols, date_weights, shock_block, flag_block, rate_block, numer_block, survive_block, start_curve, loadings, per_shard, N_TM)
        values, reverse_map = jax.vjp(runner, vols)
        gradient = reverse_map(jnp.full_like(values, NOTIONAL / PATHS))[0]
        return (vega_total + gradient, values)
    vega, values = lax.scan(one_group, jnp.zeros_like(vols), jnp.arange(N_PATHS, dtype=jnp.int32))
    return (vega, values.reshape(PATHS))
```

```python
import functools

import jax
import jax.numpy as jnp
from jax import lax
from jax.experimental import pallas as pl
from jax.experimental.pallas import tpu as pltpu
from jax.sharding import PartitionSpec as P

ACCRUAL = 0.25
STRIKE = 0.04
SMOOTHING = 0.01
NOTIONAL = 100.0
HIGHEST = lax.Precision.HIGHEST
MESH = pl.DeviceIdType.MESH
F32 = jnp.float32
BF16 = jnp.bfloat16

SHARDS = 8
PER = 5
NF = 80
VMEM_LIMIT = 60 * 1024 * 1024


def first_needed(shard):
    return max(2 * shard * PER - 1, 0)


def row_start(shard):
    return first_needed(shard) // 16 * 16


def sent_start(shard):
    return first_needed(shard) // 8 * 8


def exchange_kernel(
    width,
    shocks, bits, rates, numer, survive, vols, regress, slots,
    shocks_x, bits_x, rates_x, numer_x, survive_x, vols_x, regress_x, slots_x,
    send_sem, recv_sem, local_sem,
):
    me = lax.axis_index("tm")
    barrier = pltpu.get_barrier_semaphore()
    for step in range(1, SHARDS):
        other = lax.rem(me + step, SHARDS)
        pl.semaphore_signal(barrier, inc=1, device_id={"tm": other}, device_id_type=MESH)
    pl.semaphore_wait(barrier, SHARDS - 1)

    def cut(target):
        return pl.ds(pl.multiple_of(target * width, width), width)

    def pairs(source, target):
        return (
            (vols, vols_x.at[source]),
            (regress, regress_x.at[source]),
            (slots, slots_x.at[source]),
            (numer.at[:, cut(target)], numer_x.at[source]),
            (survive.at[:, cut(target)], survive_x.at[source]),
            (bits.at[:, cut(target)], bits_x.at[source]),
            (shocks.at[:, :, cut(target)], shocks_x.at[source]),
        )

    def rate_pair(source, target):
        top = sent_start(source + 1)
        rows = pl.ds(top, NF - top)
        return (rates.at[0, rows, cut(target)], rates_x.at[source, rows, :])

    def remote(pair, kind, source, step, target):
        return pltpu.make_async_remote_copy(
            src_ref=pair[0],
            dst_ref=pair[1],
            send_sem=send_sem.at[kind, step],
            recv_sem=recv_sem.at[kind, source],
            device_id={"tm": target},
            device_id_type=MESH,
        )

    order = (4, 3, 5, 2, 6, 1, 7)
    for step in order:
        target = lax.rem(me + step, SHARDS)
        for kind, pair in enumerate(pairs(me, target)):
            remote(pair, kind, me, step, target).start()
    for source in range(SHARDS - 1):

        @pl.when(me == source)
        def _():
            for step in order:
                target = lax.rem(me + step, SHARDS)
                remote(rate_pair(source, target), 7, source, step, target).start()

    for kind, pair in enumerate(pairs(me, me)):
        pltpu.make_async_copy(pair[0], pair[1], local_sem.at[kind]).start()
    for source in range(SHARDS - 1):

        @pl.when(me == source)
        def _():
            pair = rate_pair(source, source)
            pltpu.make_async_copy(pair[0], pair[1], local_sem.at[7]).start()

    for kind, pair in enumerate(pairs(me, me)):
        pltpu.make_async_copy(pair[0], pair[1], local_sem.at[kind]).wait()
    for source in range(SHARDS - 1):

        @pl.when(me == source)
        def _():
            pair = rate_pair(source, source)
            pltpu.make_async_copy(pair[0], pair[1], local_sem.at[7]).wait()

    for step in order:
        target = lax.rem(me + step, SHARDS)
        for kind, pair in enumerate(pairs(me, target)):
            remote(pair, kind, me, step, target).wait_send()
    for source in range(SHARDS - 1):

        @pl.when(me == source)
        def _():
            for step in order:
                target = lax.rem(me + step, SHARDS)
                remote(rate_pair(source, target), 7, source, step, target).wait_send()

    for source in range(SHARDS):

        @pl.when(me != source)
        def _():
            for kind, pair in enumerate(pairs(source, source)):
                remote(pair, kind, source, 0, source).wait_recv()
            if source < SHARDS - 1:
                remote(rate_pair(source, source), 7, source, 0, source).wait_recv()


def exchange(width, shocks, bits, rates, numer, survive, vols, regress, slots):
    anywhere = pl.BlockSpec(memory_space=pl.ANY)
    shapes = (
        ((SHARDS, PER, 4, width), F32),
        ((SHARDS, PER, width), jnp.int32),
        ((SHARDS, NF, width), F32),
        ((SHARDS, 1, width), F32),
        ((SHARDS, 1, width), F32),
        ((SHARDS, PER, NF), F32),
        ((SHARDS, PER, 6), F32),
        ((SHARDS, 1, PER), jnp.int32),
    )
    return pl.pallas_call(
        functools.partial(exchange_kernel, width),
        name="exchange",
        out_shape=[jax.ShapeDtypeStruct(s, t) for s, t in shapes],
        in_specs=[anywhere] * 8,
        out_specs=[anywhere] * 8,
        scratch_shapes=[
            pltpu.SemaphoreType.DMA((8, SHARDS)),
            pltpu.SemaphoreType.DMA((8, SHARDS)),
            pltpu.SemaphoreType.DMA((8,)),
        ],
        compiler_params=pltpu.CompilerParams(
            collective_id=0, has_side_effects=True, vmem_limit_bytes=VMEM_LIMIT
        ),
    )(shocks, bits, rates, numer, survive, vols, regress, slots)


def halves(x):
    high = x.astype(BF16)
    low = (x - high.astype(F32)).astype(BF16)
    return high, low


def compute_kernel(
    path_weight,
    curve, loads, shocks, bits, rates, numer, survive, vols, regress, slots,
    vega, value,
    square, stack, forward_lhs, backward_lhs, sums_lhs, tails_lhs, sigma, curve_wide,
    state, start, v_all, w_all, tail_all, annuity_all, last_all, growth_all, flags,
    mult_tail, mult_last, mult_numer, columns,
):
    width = value.shape[1]
    a = ACCRUAL

    def wide(x):
        return jnp.concatenate([x] * (width // 128), axis=1)

    lane = lax.broadcasted_iota(jnp.int32, (128, 128), 1)
    row = lax.broadcasted_iota(jnp.int32, (128, 128), 0)
    square[...] = jnp.zeros((128, 128), F32)
    raw = loads[...]
    unit = raw / jnp.sqrt(jnp.sum(raw * raw, axis=0, keepdims=True))
    square[0:4, 0:NF] = unit
    padded = square[...]
    turned = jnp.transpose(padded)
    full = jnp.dot(turned, padded, precision=HIGHEST, preferred_element_type=F32)

    def split_f32(x):
        high = x.astype(BF16).astype(F32)
        return high, (x - high).astype(BF16).astype(F32)

    for target, keep in ((forward_lhs, row <= lane), (backward_lhs, row >= lane)):
        high, low = split_f32(jnp.where(keep, full, 0.0))
        stack[...] = jnp.zeros((256, 128), F32)
        stack[0:NF, :] = high[:NF]
        stack[NF : 2 * NF, :] = high[:NF]
        stack[2 * NF : 3 * NF, :] = low[:NF]
        if target is forward_lhs:
            part_high, part_low = split_f32(padded)
            stack[240:244, :] = part_high[0:4]
            stack[244:248, :] = part_high[0:4]
            stack[248:252, :] = part_low[0:4]
        target[...] = jnp.transpose(stack[...])[:NF].astype(BF16)
    stack[...] = jnp.zeros((256, 128), F32)
    lower = jnp.where((row <= lane) & (row < NF), 1.0, 0.0)
    stack[0:NF, :] = lower[:NF]
    stack[NF : 2 * NF, :] = lower[:NF]
    sums_lhs[...] = jnp.transpose(stack[...])[:NF].astype(BF16)
    upper = jnp.where((row >= lane) & (row < NF), 1.0, 0.0)
    stack[0:NF, :] = upper[:NF]
    stack[NF : 2 * NF, :] = upper[:NF]
    tails_lhs[...] = jnp.transpose(stack[...])[:NF].astype(BF16)

    square[...] = jnp.zeros((128, 128), F32)
    for s in range(SHARDS):
        square[s * PER : (s + 1) * PER, 0:NF] = vols[s]
    turned = jnp.transpose(square[...])
    for s in range(SHARDS):
        top = row_start(s)
        for k in range(PER):
            d = s * PER + k
            column = jnp.broadcast_to(turned[top:NF, d : d + 1], (NF - top, 128))
            sigma[s, k, top:NF, :] = jnp.where(row[top:NF] >= 2 * d + 1, column, 0.0)
    square[...] = jnp.zeros((128, 128), F32)
    square[0:1, 0:NF] = curve[...]
    column = jnp.transpose(square[...])[:NF, 0:1]
    curve_wide[...] = jnp.broadcast_to(column, (NF, 128))

    square[...] = jnp.zeros((128, 128), F32)
    for s in range(SHARDS):
        square[s * PER : (s + 1) * PER, 0:6] = regress[s]
    ids = jnp.concatenate([slots[s] for s in range(SHARDS)], axis=0)
    hot = jnp.concatenate(
        [
            jnp.where(jnp.broadcast_to(ids[:, k : k + 1], (SHARDS, 128)) == lane[:SHARDS], 1.0, 0.0)
            for k in range(PER)
        ],
        axis=0,
    )
    weights = jnp.dot(hot, square[...], precision=HIGHEST, preferred_element_type=F32)

    for s in range(SHARDS):
        for k in range(PER):
            flags[k, s : s + 1, :] = bits[s, k : k + 1, :].astype(F32)

    for s in range(SHARDS):
        top = row_start(s)
        if s == 0:
            first = wide(curve_wide[...])
        else:
            position = lax.broadcasted_iota(jnp.int32, (NF - top, width), 0) + top
            first = jnp.where(position >= first_needed(s), rates[s - 1, top:NF, :], STRIKE)
        start[s, top:NF, :] = first
        state[s, top:NF, :] = first

    def zeros_above(top, x):
        if top == 0:
            return x
        return jnp.concatenate([jnp.zeros((top, x.shape[1]), x.dtype), x], axis=0)

    def forward(k, carry):
        for s in range(SHARDS):
            top = row_start(s)
            if s == 0:
                h = jnp.where(k == 0, a, 2.0 * a).astype(F32)
                root = jnp.where(k == 0, a**0.5, (2.0 * a) ** 0.5).astype(F32)
            else:
                h, root = 2.0 * a, (2.0 * a) ** 0.5
            current = state[s, top:NF, :]
            scaled = a * current
            v = scaled / (1.0 + scaled)
            v_all[s, k, top:NF, :] = v
            opening = 2 * (s * PER + k)
            second = 1.0 + a * state[s, pl.ds(opening, 1), :]
            if s == 0:
                before = 1.0 + a * state[s, pl.ds(jnp.maximum(opening - 1, 0), 1), :]
                before = jnp.where(k == 0, 1.0, before)
            else:
                before = 1.0 + a * state[s, pl.ds(opening - 1, 1), :]
            growth_all[k, s : s + 1, :] = before * second
            sig = wide(sigma[s, k, top:NF, :])
            hsig = h * sig
            high, low = halves(hsig * v)
            shock = root * shocks[s, k]
            shock_high = shock.astype(BF16).astype(F32)
            noise = jnp.concatenate(
                [shock_high, shock - shock_high, shock_high, jnp.zeros_like(shock)], axis=0
            ).astype(BF16)
            high, low = zeros_above(top, high), zeros_above(top, low)
            rhs = jnp.concatenate([high, low, high, noise], axis=0)
            w = jnp.dot(forward_lhs[top:NF, :], rhs, preferred_element_type=F32)
            w_all[s, k, top:NF, :] = w - hsig
            current = current * jnp.exp(sig * (w - 0.5 * hsig))
            state[s, top:NF, :] = current
            position = lax.broadcasted_iota(jnp.int32, (NF - top, width), 0) + top
            living = position > opening
            logs = jnp.where(living, jnp.log(1.0 + a * current), 0.0)
            high, low = halves(logs)
            rhs = jnp.concatenate([zeros_above(top, high), zeros_above(top, low)], axis=0)
            total = jnp.dot(sums_lhs[top:NF, 0 : 2 * NF], rhs, preferred_element_type=F32)
            bonds = jnp.where(living, jnp.exp(-total), 0.0)
            annuity_all[k, s : s + 1, :] = a * jnp.sum(bonds, axis=0, keepdims=True)
            last_all[k, s : s + 1, :] = bonds[NF - top - 1 : NF - top]
            high, low = halves(bonds)
            rhs = jnp.concatenate([zeros_above(top, high), zeros_above(top, low)], axis=0)
            tail_all[s, k, top:NF, :] = jnp.dot(
                tails_lhs[top:NF, 0 : 2 * NF], rhs, preferred_element_type=F32
            )
        return carry

    lax.fori_loop(0, PER, forward, 0)
    for s in range(SHARDS):
        top = row_start(s)
        scaled = a * state[s, top:NF, :]
        v_all[s, PER, top:NF, :] = scaled / (1.0 + scaled)

    one = jnp.ones((1, width), F32)
    numeraire = jnp.concatenate([one] + [numer[s] for s in range(SHARDS - 1)], axis=0)
    survival = jnp.concatenate([one] + [survive[s] for s in range(SHARDS - 1)], axis=0)
    scale = path_weight * NOTIONAL
    kept = []
    values = jnp.zeros((SHARDS, width), F32)
    for k in range(PER):
        numeraire = numeraire * growth_all[k]
        annuity = annuity_all[k]
        floating = 1.0 - last_all[k]
        exercise = floating - STRIKE * annuity
        inverse = 1.0 / annuity
        money = (floating * inverse - STRIKE) / SMOOTHING
        w = [
            jnp.broadcast_to(weights[k * SHARDS : (k + 1) * SHARDS, b : b + 1], (SHARDS, width))
            for b in range(6)
        ]
        slope = w[3] + money * (w[4] + money * w[5])
        continuation = w[0] + money * (w[1] + money * w[2]) + annuity * slope
        gate = 1.0 / (1.0 + jnp.exp(-(exercise - continuation) / SMOOTHING))
        chance = flags[k] * gate
        discount = 1.0 / numeraire
        paid = exercise * discount
        values = values + NOTIONAL * survival * chance * paid
        kept.append(
            dict(
                numeraire=numeraire, survival=survival, annuity=annuity, floating=floating,
                inverse=inverse, money=money, slope=slope, gate=gate, chance=chance,
                discount=discount, paid=paid,
                d_money=w[1] + 2.0 * money * w[2] + annuity * (w[4] + 2.0 * money * w[5]),
            )
        )
        survival = survival * (1.0 - chance)
    value[...] = jnp.sum(values, axis=0, keepdims=True)

    one = jnp.ones((SHARDS, width), F32)
    zero = jnp.zeros((SHARDS, width), F32)
    s_mul, s_add, n_mul, n_add = one, zero, one, zero
    for k in reversed(range(PER)):
        e = kept[k]
        left = 1.0 - e["chance"]
        gain = scale * e["chance"] * e["paid"]
        s_mul, s_add = s_mul * left, s_add * left + gain
        e["n_push"] = -e["survival"] * gain * e["discount"]
        growth = growth_all[k]
        n_mul, n_add = n_mul * growth, (n_add + e["n_push"]) * growth
    survive_end = [None] * SHARDS
    numer_end = [None] * SHARDS
    s_now = jnp.zeros((1, width), F32)
    n_now = jnp.zeros((1, width), F32)
    for s in reversed(range(SHARDS)):
        survive_end[s] = s_now
        numer_end[s] = n_now
        s_now = s_mul[s : s + 1] * s_now + s_add[s : s + 1]
        n_now = n_mul[s : s + 1] * n_now + n_add[s : s + 1]
    d_survive = jnp.concatenate(survive_end, axis=0)
    d_numer = jnp.concatenate(numer_end, axis=0)
    for k in reversed(range(PER)):
        e = kept[k]
        d_numer = d_numer + e["n_push"]
        mult_numer[k] = d_numer * e["numeraire"]
        d_numer = d_numer * growth_all[k]
        d_chance = e["survival"] * (scale * e["paid"] - d_survive)
        d_score = d_chance * e["chance"] * (1.0 - e["gate"]) / SMOOTHING
        d_exercise = scale * e["survival"] * e["chance"] * e["discount"] + d_score
        d_money = -d_score * e["d_money"] / SMOOTHING
        ratio = d_money * e["inverse"]
        d_annuity = -d_score * e["slope"] - STRIKE * d_exercise - ratio * e["floating"] * e["inverse"]
        d_floating = d_exercise + ratio
        mult_tail[k] = -a * d_annuity
        mult_last[k] = d_floating * last_all[k]
        d_survive = d_survive * (1.0 - e["chance"]) + scale * e["chance"] * e["paid"]

    columns[...] = jnp.zeros((NF, 128), F32)
    pull = jnp.zeros((NF, width), F32)
    for s in reversed(range(SHARDS)):
        top = row_start(s)
        count = NF - top
        position = lax.broadcasted_iota(jnp.int32, (count, width), 0) + top
        lanes = lax.broadcasted_iota(jnp.int32, (count, 128), 1)
        if s < SHARDS - 1:
            below = row_start(s + 1)
            ratio = state[s, below:NF, :] / start[s + 1, below:NF, :]
            pull = zeros_above(below - top, pull[below - (NF - pull.shape[0]) :] * ratio)
        else:
            pull = pull[top:]

        def backward(step, pull):
            k = PER - 1 - step
            opening = 2 * (s * PER + k)
            h = 2.0 * a
            if s == 0:
                h = jnp.where(k == 0, a, 2.0 * a).astype(F32)
            sig = wide(sigma[s, k, top:NF, :])
            v = v_all[s, k, top:NF, :]
            later = v_all[s, k + 1, top:NF, :]
            push = mult_last[k, s : s + 1, :] + mult_tail[k, s : s + 1, :] * tail_all[s, k, top:NF, :]
            y = pull + jnp.where(position > opening, later * push, 0.0)
            high, low = halves(h * sig * y)
            high, low = zeros_above(top, high), zeros_above(top, low)
            rhs = jnp.concatenate([high, low, high], axis=0)
            du = jnp.dot(backward_lhs[top:NF, 0 : 3 * NF], rhs, preferred_element_type=F32)
            duv = du * v
            grown = v * mult_numer[k, s : s + 1, :]
            fixed = (position == opening) | (position == opening - 1)
            out = y + sig * duv * (1.0 - v) + jnp.where(fixed, grown, 0.0)
            by_vol = jnp.where(position > opening, y * w_all[s, k, top:NF, :] + duv, 0.0)
            summed = jnp.sum(by_vol, axis=1, keepdims=True)
            columns[top:NF, :] = jnp.where(lanes == s * PER + k, summed, columns[top:NF, :])
            return out

        pull = lax.fori_loop(0, PER, backward, pull)

    square[...] = jnp.zeros((128, 128), F32)
    square[0:NF, :] = columns[...]
    final = jnp.transpose(square[...])
    for s in range(SHARDS):
        vega[s] = final[s * PER : (s + 1) * PER, :]


def compute(path_weight, width, *arrays):
    inside = pl.BlockSpec(memory_space=pltpu.VMEM)
    big = pltpu.VMEM((SHARDS, PER, NF, width), F32)
    small = pltpu.VMEM((PER, SHARDS, width), F32)
    lhs = pltpu.VMEM((NF, 256), BF16)
    return pl.pallas_call(
        functools.partial(compute_kernel, path_weight),
        name="compute",
        out_shape=[
            jax.ShapeDtypeStruct((SHARDS, PER, 128), F32),
            jax.ShapeDtypeStruct((1, width), F32),
        ],
        in_specs=[inside] * len(arrays),
        out_specs=[inside] * 2,
        scratch_shapes=[
            pltpu.VMEM((128, 128), F32),
            pltpu.VMEM((256, 128), F32),
            lhs, lhs, lhs, lhs,
            pltpu.VMEM((SHARDS, PER, NF, 128), F32),
            pltpu.VMEM((NF, 128), F32),
            pltpu.VMEM((SHARDS, NF, width), F32),
            pltpu.VMEM((SHARDS, NF, width), F32),
            pltpu.VMEM((SHARDS, PER + 1, NF, width), F32),
            big, big,
            small, small, small, small,
            small, small, small,
            pltpu.VMEM((NF, 128), F32),
        ],
        compiler_params=pltpu.CompilerParams(vmem_limit_bytes=VMEM_LIMIT),
    )(*arrays)


def reduce_kernel(
    groups, width,
    part, value, vega, values,
    landed, values_landed, summed, spread,
    send_sem, recv_sem, value_send, value_recv, spread_send, spread_recv,
):
    me = lax.axis_index("tm")
    group = lax.axis_index("paths")
    barrier = pltpu.get_barrier_semaphore()
    for step in range(1, SHARDS):
        other = lax.rem(me + step, SHARDS)
        pl.semaphore_signal(barrier, inc=1, device_id={"tm": other}, device_id_type=MESH)
    for step in range(1, groups):
        other = lax.rem(group + step, groups)
        pl.semaphore_signal(barrier, inc=1, device_id={"paths": other}, device_id_type=MESH)
    pl.semaphore_wait(barrier, SHARDS - 1 + groups - 1)

    def block(step, source, target):
        return pltpu.make_async_remote_copy(
            src_ref=part.at[target], dst_ref=landed.at[source],
            send_sem=send_sem.at[step], recv_sem=recv_sem.at[source],
            device_id={"tm": target}, device_id_type=MESH,
        )

    def line(step, source, target):
        return pltpu.make_async_remote_copy(
            src_ref=value, dst_ref=values_landed.at[source],
            send_sem=value_send.at[step], recv_sem=value_recv.at[source],
            device_id={"tm": target}, device_id_type=MESH,
        )

    def share(step, source, target):
        return pltpu.make_async_remote_copy(
            src_ref=summed, dst_ref=spread.at[source],
            send_sem=spread_send.at[step], recv_sem=spread_recv.at[source],
            device_id={"paths": target}, device_id_type=MESH,
        )

    order = (4, 3, 5, 2, 6, 1, 7)
    for step in order:
        block(step, me, lax.rem(me + step, SHARDS)).start()
    for step in order:
        line(step, me, lax.rem(me + step, SHARDS)).start()
    landed[me] = part[me]
    values_landed[me] = value[...]
    for source in range(SHARDS):

        @pl.when(me != source)
        def _():
            block(0, source, source).wait_recv()

    total = landed[0]
    for source in range(1, SHARDS):
        total = total + landed[source]
    summed[...] = total
    spread[group] = total
    for source in range(SHARDS):

        @pl.when(me != source)
        def _():
            line(0, source, source).wait_recv()

    for step in range(1, groups):
        share(step, group, lax.rem(group + step, groups)).start()
    for source in range(SHARDS):
        values[0:1, source * width : (source + 1) * width] = values_landed[source]
    for step in order:
        block(step, me, lax.rem(me + step, SHARDS)).wait_send()
        line(step, me, lax.rem(me + step, SHARDS)).wait_send()
    for step in range(1, groups):
        share(step, group, lax.rem(group + step, groups)).wait_send()
    for step in range(1, groups):
        source = lax.rem(group + step, groups)
        share(0, source, source).wait_recv()
    total = spread[0]
    for source in range(1, groups):
        total = total + spread[source]
    vega[...] = total[:, 0:NF]


def reduce(groups, width, part, value):
    inside = pl.BlockSpec(memory_space=pltpu.VMEM)
    return pl.pallas_call(
        functools.partial(reduce_kernel, groups, width),
        name="reduce",
        out_shape=[
            jax.ShapeDtypeStruct((PER, NF), F32),
            jax.ShapeDtypeStruct((1, SHARDS * width), F32),
        ],
        in_specs=[inside] * 2,
        out_specs=[inside] * 2,
        scratch_shapes=[
            pltpu.VMEM((SHARDS, PER, 128), F32),
            pltpu.VMEM((SHARDS, 1, width), F32),
            pltpu.VMEM((PER, 128), F32),
            pltpu.VMEM((groups, PER, 128), F32),
            pltpu.SemaphoreType.DMA((SHARDS,)),
            pltpu.SemaphoreType.DMA((SHARDS,)),
            pltpu.SemaphoreType.DMA((SHARDS,)),
            pltpu.SemaphoreType.DMA((SHARDS,)),
            pltpu.SemaphoreType.DMA((groups,)),
            pltpu.SemaphoreType.DMA((groups,)),
        ],
        compiler_params=pltpu.CompilerParams(collective_id=1, has_side_effects=True),
    )(part, value)


def local(
    start_curve, loadings, vols, shocks, exercise_bits, regress, date_slot,
    ck_rates, ck_numer, ck_survive,
):
    groups = lax.axis_size("paths")
    path_count = shocks.shape[2]
    width = path_count // SHARDS
    path_weight = NOTIONAL / (path_count * groups)
    gathered = exchange(
        width, shocks, exercise_bits, ck_rates, ck_numer, ck_survive, vols, regress,
        date_slot.reshape(1, PER),
    )
    part, value = compute(
        path_weight, width, start_curve.reshape(1, NF), loadings, *gathered
    )
    vega, values = reduce(groups, width, part, value)
    return (vega, values.reshape(path_count))


def solution(mesh):
    return jax.shard_map(
        local,
        mesh=mesh,
        in_specs=(
            P(),
            P(),
            P("tm", None),
            P("tm", None, "paths"),
            P("tm", "paths"),
            P("tm", None),
            P("tm"),
            P("tm", None, "paths"),
            P("tm", "paths"),
            P("tm", "paths"),
        ),
        out_specs=(P("tm", None), P("paths")),
        check_vma=False,
    )
```

```python
import functools

import jax
import jax.numpy as jnp
from jax import lax
from jax.experimental import pallas as pl
from jax.experimental.pallas import tpu as pltpu
from jax.sharding import PartitionSpec as P

ACCRUAL = 0.25
STRIKE = 0.04
SMOOTHING = 0.01
NOTIONAL = 100.0
HIGHEST = lax.Precision.HIGHEST
MESH = pl.DeviceIdType.MESH
F32 = jnp.float32
BF16 = jnp.bfloat16

SHARDS = 8
PER = 5
NF = 80
VMEM_LIMIT = 60 * 1024 * 1024


def first_needed(shard):
    return max(2 * shard * PER - 1, 0)


def row_start(shard):
    return first_needed(shard) // 16 * 16


def sent_start(shard):
    return first_needed(shard) // 8 * 8

PHASES = (((0, 4, 5, 6, 7), (4, 5, 6, 7)), ((1, 2, 3), (0, 1, 2, 3)))
ORDER = (4, 3, 5, 2, 6, 1, 7)
KINDS = 8


def halves(x):
    high = x.astype(BF16)
    low = (x - high.astype(F32)).astype(BF16)
    return high, low


def split_f32(x):
    high = x.astype(BF16).astype(F32)
    return high, (x - high).astype(BF16).astype(F32)


def zeros_above(top, x):
    if top == 0:
        return x
    return jnp.concatenate([jnp.zeros((top, x.shape[1]), x.dtype), x], axis=0)


class Scratch:
    pass


def constants(c, loads, curve):
    lane = lax.broadcasted_iota(jnp.int32, (128, 128), 1)
    row = lax.broadcasted_iota(jnp.int32, (128, 128), 0)
    c.square[...] = jnp.zeros((128, 128), F32)
    raw = loads[...]
    c.square[0:4, 0:NF] = raw / jnp.sqrt(jnp.sum(raw * raw, axis=0, keepdims=True))
    padded = c.square[...]
    turned = jnp.transpose(padded)
    full = jnp.dot(turned, padded, precision=HIGHEST, preferred_element_type=F32)
    part_high, part_low = split_f32(padded)

    high, low = split_f32(jnp.where(row <= lane, full, 0.0))
    c.stack[...] = jnp.zeros((256, 128), F32)
    c.stack[0:NF, :] = high[:NF]
    c.stack[NF : 2 * NF, :] = high[:NF]
    c.stack[2 * NF : 3 * NF, :] = low[:NF]
    c.stack[240:244, :] = part_high[0:4]
    c.stack[244:248, :] = part_high[0:4]
    c.stack[248:252, :] = part_low[0:4]
    c.forward_lhs[...] = jnp.transpose(c.stack[...])[:NF].astype(BF16)

    high, low = split_f32(jnp.where(row >= lane, full, 0.0))
    c.stack[...] = jnp.zeros((256, 128), F32)
    c.stack[0:NF, :] = high[:NF]
    c.stack[NF : 2 * NF, :] = low[:NF]
    c.backward_lhs[...] = jnp.transpose(c.stack[...])[:NF].astype(BF16)

    lower = jnp.where((row <= lane) & (row < NF), 1.0, 0.0)
    c.stack[0:NF, :] = lower[:NF]
    c.stack[NF : 2 * NF, :] = lower[:NF]
    c.sums_lhs[...] = jnp.transpose(c.stack[...])[:NF].astype(BF16)
    upper = jnp.where((row >= lane) & (row < NF), 1.0, 0.0)
    c.stack[0:NF, :] = upper[:NF]
    c.stack[NF : 2 * NF, :] = upper[:NF]
    c.tails_lhs[...] = jnp.transpose(c.stack[...])[:NF].astype(BF16)

    c.square[...] = jnp.zeros((128, 128), F32)
    c.square[0:1, 0:NF] = curve[...]
    column = jnp.transpose(c.square[...])[:NF, 0:1]
    c.start[0][...] = jnp.broadcast_to(column, (NF, c.width))


def tables(c):
    lane = lax.broadcasted_iota(jnp.int32, (SHARDS, 128), 1)
    row = lax.broadcasted_iota(jnp.int32, (128, 128), 0)
    c.square[...] = jnp.zeros((128, 128), F32)
    for s in range(SHARDS):
        c.square[s * PER : (s + 1) * PER, 0:NF] = c.vols[s]
    turned = jnp.transpose(c.square[...])
    for s in range(SHARDS):
        top = row_start(s)
        for k in range(PER):
            d = s * PER + k
            column = jnp.broadcast_to(turned[top:NF, d : d + 1], (NF - top, 128))
            c.sigma[s, k, top:NF, :] = jnp.where(row[top:NF] >= 2 * d + 1, column, 0.0)
    c.square[...] = jnp.zeros((128, 128), F32)
    for s in range(SHARDS):
        c.square[s * PER : (s + 1) * PER, 0:6] = c.regress[s]
    ids = jnp.concatenate([c.slots[s] for s in range(SHARDS)], axis=0)
    hot = jnp.concatenate(
        [
            jnp.where(jnp.broadcast_to(ids[:, k : k + 1], (SHARDS, 128)) == lane, 1.0, 0.0)
            for k in range(PER)
        ],
        axis=0,
    )
    c.weights[...] = jnp.dot(hot, c.square[...], precision=HIGHEST, preferred_element_type=F32)


def flag_rows(c):
    for s in range(SHARDS):
        for k in range(PER):
            c.flags[k, s : s + 1, :] = c.bits[s, k : k + 1, :].astype(F32)


def forward_pass(c, shards):
    a, width = ACCRUAL, c.width

    def wide(x):
        return jnp.concatenate([x] * (width // 128), axis=1)

    for s in shards:
        top = row_start(s)
        if s > 0:
            position = lax.broadcasted_iota(jnp.int32, (NF - top, width), 0) + top
            c.start[s][top:NF, :] = jnp.where(
                position >= first_needed(s), c.rates[s - 1, top:NF, :], STRIKE
            )
        c.state[s][top:NF, :] = c.start[s][top:NF, :]

    def drift(s, k, held):
        top = row_start(s)
        if s == 0:
            h = jnp.where(k == 0, a, 2.0 * a).astype(F32)
            root = jnp.where(k == 0, a**0.5, (2.0 * a) ** 0.5).astype(F32)
        else:
            h, root = 2.0 * a, (2.0 * a) ** 0.5
        current = c.state[s][top:NF, :]
        opening = 2 * (s * PER + k)
        second = 1.0 + a * c.state[s][pl.ds(opening, 1), :]
        if s == 0:
            before = 1.0 + a * c.state[s][pl.ds(jnp.maximum(opening - 1, 0), 1), :]
            before = jnp.where(k == 0, 1.0, before)
        else:
            before = 1.0 + a * c.state[s][pl.ds(opening - 1, 1), :]
        c.growth[k, s : s + 1, :] = before * second
        scaled = a * current
        v = scaled / (1.0 + scaled)
        c.v[s][k, top:NF, :] = v
        sig = wide(c.sigma[s, k, top:NF, :])
        hsig = h * sig
        high, low = halves(hsig * v)
        shock = root * c.shocks[s, k]
        shock_high = shock.astype(BF16).astype(F32)
        noise = jnp.concatenate(
            [shock_high, shock - shock_high, shock_high, jnp.zeros_like(shock)], axis=0
        ).astype(BF16)
        high, low = zeros_above(top, high), zeros_above(top, low)
        rhs = jnp.concatenate([high, low, high, noise], axis=0)
        w = jnp.dot(c.forward_lhs[top:NF, :], rhs, preferred_element_type=F32)
        held[s] = (w, sig, hsig, current)

    def moved(s, k, held):
        top = row_start(s)
        w, sig, hsig, current = held[s]
        c.w[s][k, top:NF, :] = w - hsig
        current = current * jnp.exp(sig * (w - 0.5 * hsig))
        c.state[s][top:NF, :] = current
        position = lax.broadcasted_iota(jnp.int32, (NF - top, width), 0) + top
        living = position > 2 * (s * PER + k)
        logs = jnp.where(living, jnp.log(1.0 + a * current), 0.0)
        high, low = halves(logs)
        rhs = jnp.concatenate([zeros_above(top, high), zeros_above(top, low)], axis=0)
        total = jnp.dot(c.sums_lhs[top:NF, 0 : 2 * NF], rhs, preferred_element_type=F32)
        held[s] = (total, living)

    def bonds_of(s, k, held):
        top = row_start(s)
        total, living = held[s]
        bonds = jnp.where(living, jnp.exp(-total), 0.0)
        c.annuity[k, s : s + 1, :] = a * jnp.sum(bonds, axis=0, keepdims=True)
        c.last[k, s : s + 1, :] = bonds[NF - top - 1 : NF - top]
        high, low = halves(bonds)
        rhs = jnp.concatenate([zeros_above(top, high), zeros_above(top, low)], axis=0)
        c.tail[s][k, top:NF, :] = jnp.dot(
            c.tails_lhs[top:NF, 0 : 2 * NF], rhs, preferred_element_type=F32
        )

    def forward(k, carry):
        held = {}
        count = len(shards)
        for step in range(count + 2):
            if step >= 2:
                bonds_of(shards[step - 2], k, held)
            if 1 <= step <= count:
                moved(shards[step - 1], k, held)
            if step < count:
                drift(shards[step], k, held)
        return carry

    lax.fori_loop(0, PER, forward, 0)
    for s in shards:
        top = row_start(s)
        scaled = a * c.state[s][top:NF, :]
        c.v[s][PER, top:NF, :] = scaled / (1.0 + scaled)


def exercise_pass(c, shards, s_now, n_now):
    a, width = ACCRUAL, c.width
    low, count = shards[0], len(shards)
    rows = slice(low, low + count)

    def starts(ref):
        lines = [ref[s - 1] if s > 0 else jnp.ones((1, width), F32) for s in shards]
        return jnp.concatenate(lines, axis=0)

    numeraire, survival = starts(c.numer), starts(c.survive)
    scale = c.path_weight * NOTIONAL
    kept = []
    values = jnp.zeros((count, width), F32)
    for k in range(PER):
        growth = c.growth[k, rows, :]
        numeraire = numeraire * growth
        annuity = c.annuity[k, rows, :]
        last = c.last[k, rows, :]
        floating = 1.0 - last
        exercise = floating - STRIKE * annuity
        inverse = 1.0 / annuity
        money = (floating * inverse - STRIKE) / SMOOTHING
        w = [
            jnp.broadcast_to(
                c.weights[k * SHARDS + low : k * SHARDS + low + count, b : b + 1], (count, width)
            )
            for b in range(6)
        ]
        slope = w[3] + money * (w[4] + money * w[5])
        continuation = w[0] + money * (w[1] + money * w[2]) + annuity * slope
        gate = 1.0 / (1.0 + jnp.exp(-(exercise - continuation) / SMOOTHING))
        chance = c.flags[k, rows, :] * gate
        discount = 1.0 / numeraire
        paid = exercise * discount
        values = values + NOTIONAL * survival * chance * paid
        kept.append(
            dict(
                numeraire=numeraire, survival=survival, floating=floating, growth=growth,
                last=last, inverse=inverse, slope=slope, gate=gate, chance=chance,
                discount=discount, paid=paid,
                d_money=w[1] + 2.0 * money * w[2] + annuity * (w[4] + 2.0 * money * w[5]),
            )
        )
        survival = survival * (1.0 - chance)

    one, zero = jnp.ones((count, width), F32), jnp.zeros((count, width), F32)
    s_mul, s_add, n_mul, n_add = one, zero, one, zero
    for k in reversed(range(PER)):
        e = kept[k]
        left = 1.0 - e["chance"]
        gain = scale * e["chance"] * e["paid"]
        s_mul, s_add = s_mul * left, s_add * left + gain
        e["n_push"] = -e["survival"] * gain * e["discount"]
        n_mul, n_add = n_mul * e["growth"], (n_add + e["n_push"]) * e["growth"]
    survive_end, numer_end = [None] * count, [None] * count
    for i in reversed(range(count)):
        survive_end[i], numer_end[i] = s_now, n_now
        s_now = s_mul[i : i + 1] * s_now + s_add[i : i + 1]
        n_now = n_mul[i : i + 1] * n_now + n_add[i : i + 1]
    d_survive = jnp.concatenate(survive_end, axis=0)
    d_numer = jnp.concatenate(numer_end, axis=0)
    for k in reversed(range(PER)):
        e = kept[k]
        d_numer = d_numer + e["n_push"]
        c.mult_numer[k, rows, :] = d_numer * e["numeraire"]
        d_numer = d_numer * e["growth"]
        d_chance = e["survival"] * (scale * e["paid"] - d_survive)
        d_score = d_chance * e["chance"] * (1.0 - e["gate"]) / SMOOTHING
        d_exercise = scale * e["survival"] * e["chance"] * e["discount"] + d_score
        d_money = -d_score * e["d_money"] / SMOOTHING
        ratio = d_money * e["inverse"]
        d_annuity = -d_score * e["slope"] - STRIKE * d_exercise - ratio * e["floating"] * e["inverse"]
        d_floating = d_exercise + ratio
        c.mult_tail[k, rows, :] = -a * d_annuity
        c.mult_last[k, rows, :] = d_floating * e["last"]
        d_survive = d_survive * (1.0 - e["chance"]) + scale * e["chance"] * e["paid"]
    return s_now, n_now, jnp.sum(values, axis=0, keepdims=True)


def backward_shard(c, s, pull):
    a, width = ACCRUAL, c.width
    top = row_start(s)
    count = NF - top
    position = lax.broadcasted_iota(jnp.int32, (count, width), 0) + top
    if s < SHARDS - 1:
        below = row_start(s + 1)
        ratio = c.state[s][below:NF, :] / c.start[s + 1][below:NF, :]
        pull = zeros_above(below - top, pull * ratio)

    def backward(step, pull):
        k = PER - 1 - step
        opening = 2 * (s * PER + k)
        h = 2.0 * a
        if s == 0:
            h = jnp.where(k == 0, a, 2.0 * a).astype(F32)
        narrow = c.sigma[s, k, top:NF, :]
        sig = jnp.concatenate([narrow] * (width // 128), axis=1)
        v = c.v[s][k, top:NF, :]
        push = c.mult_last[k, s : s + 1, :] + c.mult_tail[k, s : s + 1, :] * c.tail[s][k, top:NF, :]
        y = pull + jnp.where(position > opening, c.v[s][k + 1, top:NF, :] * push, 0.0)
        part = zeros_above(top, (h * sig * y).astype(BF16))
        rhs = jnp.concatenate([part, part], axis=0)
        du = jnp.dot(c.backward_lhs[top:NF, 0 : 2 * NF], rhs, preferred_element_type=F32)
        fixed = (position == opening) | (position == opening - 1)
        base = y + jnp.where(fixed, v * c.mult_numer[k, s : s + 1, :], 0.0)
        factor = sig * (v * (1.0 - v))
        out = base + factor * du
        by_vol = jnp.where(position > opening, y * c.w[s][k, top:NF, :] + du * v, 0.0)
        folded = by_vol[:, 0:128]
        for piece in range(1, width // 128):
            folded = folded + by_vol[:, piece * 128 : (piece + 1) * 128]
        c.by_vol[s][k, top:NF, :] = folded
        return out

    return lax.fori_loop(0, PER, backward, pull, unroll=UNROLL)


def sum_paths(c, shards):
    for s in shards:
        top = row_start(s)
        lanes = lax.broadcasted_iota(jnp.int32, (NF - top, 128), 1)
        gathered = c.square[top:NF, :]
        for k in range(PER):
            summed = jnp.sum(c.by_vol[s][k, top:NF, :], axis=1, keepdims=True)
            gathered = jnp.where(lanes == s * PER + k, summed, gathered)
        c.square[top:NF, :] = gathered


UNROLL = True


def kernel(
    path_weight, groups,
    curve, loads, shocks, bits, rates, numer, survive, vols, regress, slots,
    vega, values,
    shocks_x, bits_x, rates_x, numer_x, survive_x, vols_x, regress_x, slots_x,
    square, stack, forward_lhs, backward_lhs, sums_lhs, tails_lhs, sigma, weights,
    growth, annuity, last, flags, mult_tail, mult_last, mult_numer,
    part, landed, value, values_landed, summed, spread,
    *rest,
):
    per_shard, sems = rest[: 7 * SHARDS], rest[7 * SHARDS :]
    (send_sem, recv_sem, local_sem, part_send, part_recv, value_send, value_recv,
     spread_send, spread_recv) = sems
    c = Scratch()
    c.path_weight, c.width = path_weight, shocks_x.shape[3]
    c.shocks, c.bits, c.rates, c.numer, c.survive = shocks_x, bits_x, rates_x, numer_x, survive_x
    c.vols, c.regress, c.slots = vols_x, regress_x, slots_x
    c.square, c.stack, c.sigma, c.weights = square, stack, sigma, weights
    c.forward_lhs, c.backward_lhs = forward_lhs, backward_lhs
    c.sums_lhs, c.tails_lhs = sums_lhs, tails_lhs
    c.growth, c.annuity, c.last, c.flags = growth, annuity, last, flags
    c.mult_tail, c.mult_last, c.mult_numer = mult_tail, mult_last, mult_numer
    c.state, c.start, c.v, c.w, c.tail, c.by_vol, _ = (
        per_shard[i * SHARDS : (i + 1) * SHARDS] for i in range(7)
    )
    width = c.width
    me = lax.axis_index("tm")
    group = lax.axis_index("paths")

    barrier = pltpu.get_barrier_semaphore()
    for step in ORDER:
        other = lax.rem(me + step, SHARDS)
        pl.semaphore_signal(barrier, inc=1, device_id={"tm": other}, device_id_type=MESH)
    for step in range(1, groups):
        other = lax.rem(group + step, groups)
        pl.semaphore_signal(barrier, inc=1, device_id={"paths": other}, device_id_type=MESH)

    def cut(target):
        return pl.ds(pl.multiple_of(target * width, width), width)

    def pair_of(kind, source, target):
        if kind == 0:
            return vols, vols_x.at[source]
        if kind == 1:
            return regress, regress_x.at[source]
        if kind == 2:
            return slots, slots_x.at[source]
        if kind == 3:
            return shocks.at[:, :, cut(target)], shocks_x.at[source]
        if kind == 4:
            return bits.at[:, cut(target)], bits_x.at[source]
        if kind == 5:
            return numer.at[:, cut(target)], numer_x.at[source]
        if kind == 6:
            return survive.at[:, cut(target)], survive_x.at[source]
        top = sent_start(source + 1)
        rows = pl.ds(top, NF - top)
        return rates.at[0, rows, cut(target)], rates_x.at[source, rows, :]

    def here(kind, source):
        src, dst = pair_of(kind, source, source)
        return pltpu.make_async_copy(src, dst, local_sem.at[kind])

    def remote(kind, source, step, target):
        src, dst = pair_of(kind, source, target)
        return pltpu.make_async_remote_copy(
            src_ref=src, dst_ref=dst,
            send_sem=send_sem.at[kind, step], recv_sem=recv_sem.at[kind, source],
            device_id={"tm": target}, device_id_type=MESH,
        )

    def rates_by_source(action):
        for source in range(SHARDS - 1):

            @pl.when(me == source)
            def _():
                action(source)

    def start_rates(source):
        for step in ORDER:
            remote(7, source, step, lax.rem(me + step, SHARDS)).start()

    def end_rates(source):
        for step in ORDER:
            remote(7, source, step, lax.rem(me + step, SHARDS)).wait_send()

    def await_kinds(kinds, sources):
        for source in sources:

            @pl.when(me != source)
            def _():
                for kind in kinds:
                    remote(kind, source, 0, source).wait_recv()

            @pl.when(me == source)
            def _():
                for kind in kinds:
                    here(kind, source).wait()

    for kind in range(7):
        here(kind, me).start()
    rates_by_source(lambda source: here(7, source).start())
    constants(c, loads, curve)
    pl.semaphore_wait(barrier, SHARDS - 1 + groups - 1)
    for kinds in ((0, 1, 2), (3, 4, 5, 6)):
        for step in ORDER:
            for kind in kinds:
                remote(kind, me, step, lax.rem(me + step, SHARDS)).start()
    rates_by_source(start_rates)

    everyone = range(SHARDS)
    await_kinds((0, 1, 2), everyone)
    tables(c)
    await_kinds((3, 4, 5, 6), everyone)
    flag_rows(c)

    s_now = jnp.zeros((1, width), F32)
    n_now = jnp.zeros((1, width), F32)
    pull = jnp.zeros((NF - row_start(SHARDS - 1), width), F32)
    paid = None
    square[...] = jnp.zeros((128, 128), F32)
    for first_shards, shards in PHASES:
        await_kinds((7,), [s - 1 for s in reversed(first_shards) if s > 0])
        forward_pass(c, first_shards)
        s_now, n_now, gains = exercise_pass(c, shards, s_now, n_now)
        paid = gains if paid is None else paid + gains
        if shards[0] == 0:
            value[...] = paid
        for s in reversed(shards):
            pull = backward_shard(c, s, pull)
        sum_paths(c, shards)

    turned = jnp.transpose(square[...])
    for s in range(SHARDS):
        part[s] = turned[s * PER : (s + 1) * PER, :]

    def block(step, source, target):
        return pltpu.make_async_remote_copy(
            src_ref=part.at[target], dst_ref=landed.at[source],
            send_sem=part_send.at[step], recv_sem=part_recv.at[source],
            device_id={"tm": target}, device_id_type=MESH,
        )

    def line(step, source, target):
        return pltpu.make_async_remote_copy(
            src_ref=value, dst_ref=values_landed.at[source],
            send_sem=value_send.at[step], recv_sem=value_recv.at[source],
            device_id={"tm": target}, device_id_type=MESH,
        )

    def share(step, source, target):
        return pltpu.make_async_remote_copy(
            src_ref=summed, dst_ref=spread.at[source],
            send_sem=spread_send.at[step], recv_sem=spread_recv.at[source],
            device_id={"paths": target}, device_id_type=MESH,
        )

    for step in ORDER:
        line(step, me, lax.rem(me + step, SHARDS)).start()
    for step in ORDER:
        block(step, me, lax.rem(me + step, SHARDS)).start()
    landed[me] = part[me]
    values_landed[me] = value[...]
    for kind in range(7):
        for step in ORDER:
            remote(kind, me, step, lax.rem(me + step, SHARDS)).wait_send()
    rates_by_source(end_rates)
    for source in everyone:

        @pl.when(me != source)
        def _():
            block(0, source, source).wait_recv()

    total = landed[0]
    for source in range(1, SHARDS):
        total = total + landed[source]
    summed[...] = total
    spread[group] = total
    for source in everyone:

        @pl.when(me != source)
        def _():
            line(0, source, source).wait_recv()

    for step in range(1, groups):
        share(step, group, lax.rem(group + step, groups)).start()
    for source in everyone:
        values[0:1, source * width : (source + 1) * width] = values_landed[source]
    for step in ORDER:
        block(step, me, lax.rem(me + step, SHARDS)).wait_send()
        line(step, me, lax.rem(me + step, SHARDS)).wait_send()
    for step in range(1, groups):
        share(step, group, lax.rem(group + step, groups)).wait_send()
    for step in range(1, groups):
        source = lax.rem(group + step, groups)
        share(0, source, source).wait_recv()
    total = spread[0]
    for source in range(1, groups):
        total = total + spread[source]
    vega[...] = total[:, 0:NF]


def local(
    start_curve, loadings, vols, shocks, exercise_bits, regress, date_slot,
    ck_rates, ck_numer, ck_survive,
):
    groups = lax.axis_size("paths")
    path_count = shocks.shape[2]
    width = path_count // SHARDS
    inside = pl.BlockSpec(memory_space=pltpu.VMEM)
    anywhere = pl.BlockSpec(memory_space=pl.ANY)
    small = pltpu.VMEM((PER, SHARDS, width), F32)
    lhs = pltpu.VMEM((NF, 256), BF16)
    plane = pltpu.VMEM((NF, width), F32)
    dates = pltpu.VMEM((PER, NF, width), F32)
    dma = pltpu.SemaphoreType.DMA
    vega, values = pl.pallas_call(
        functools.partial(kernel, NOTIONAL / (path_count * groups), groups),
        name="pathwise_vega",
        out_shape=[
            jax.ShapeDtypeStruct((PER, NF), F32),
            jax.ShapeDtypeStruct((1, path_count), F32),
        ],
        in_specs=[inside] * 2 + [anywhere] * 8,
        out_specs=[inside] * 2,
        scratch_shapes=[
            pltpu.VMEM((SHARDS, PER, 4, width), F32),
            pltpu.VMEM((SHARDS, PER, width), jnp.int32),
            pltpu.VMEM((SHARDS, NF, width), F32),
            pltpu.VMEM((SHARDS, 1, width), F32),
            pltpu.VMEM((SHARDS, 1, width), F32),
            pltpu.VMEM((SHARDS, PER, NF), F32),
            pltpu.VMEM((SHARDS, PER, 6), F32),
            pltpu.VMEM((SHARDS, 1, PER), jnp.int32),
            pltpu.VMEM((128, 128), F32),
            pltpu.VMEM((256, 128), F32),
            lhs, lhs, lhs, lhs,
            pltpu.VMEM((SHARDS, PER, NF, 128), F32),
            pltpu.VMEM((PER * SHARDS, 128), F32),
            small, small, small, small,
            small, small, small,
            pltpu.VMEM((SHARDS, PER, 128), F32),
            pltpu.VMEM((SHARDS, PER, 128), F32),
            pltpu.VMEM((1, width), F32),
            pltpu.VMEM((SHARDS, 1, width), F32),
            pltpu.VMEM((PER, 128), F32),
            pltpu.VMEM((groups, PER, 128), F32),
        ]
        + [plane] * SHARDS
        + [plane] * SHARDS
        + [pltpu.VMEM((PER + 1, NF, width), F32)] * SHARDS
        + [dates] * SHARDS
        + [dates] * SHARDS
        + [pltpu.VMEM((PER, NF, 128), F32)] * SHARDS
        + [pltpu.VMEM((8, 128), F32)] * SHARDS
        + [
            dma((KINDS, SHARDS)), dma((KINDS, SHARDS)), dma((KINDS,)),
            dma((SHARDS,)), dma((SHARDS,)), dma((SHARDS,)), dma((SHARDS,)),
            dma((groups,)), dma((groups,)),
        ],
        compiler_params=pltpu.CompilerParams(
            collective_id=0, has_side_effects=True, vmem_limit_bytes=VMEM_LIMIT
        ),
    )(
        start_curve.reshape(1, NF), loadings, shocks, exercise_bits, ck_rates, ck_numer,
        ck_survive, vols, regress, date_slot.reshape(1, PER),
    )
    return (vega, values.reshape(path_count))


def solution(mesh):
    return jax.shard_map(
        local,
        mesh=mesh,
        in_specs=(
            P(),
            P(),
            P("tm", None),
            P("tm", None, "paths"),
            P("tm", "paths"),
            P("tm", None),
            P("tm"),
            P("tm", None, "paths"),
            P("tm", "paths"),
            P("tm", "paths"),
        ),
        out_specs=(P("tm", None), P("paths")),
        check_vma=False,
    )
```

```python
import functools

import jax
import jax.numpy as jnp
from jax import lax
from jax.experimental import pallas as pl
from jax.experimental.pallas import tpu as pltpu
from jax.sharding import PartitionSpec as P

ACCRUAL = 0.25
STRIKE = 0.04
SMOOTHING = 0.01
NOTIONAL = 100.0
HIGHEST = lax.Precision.HIGHEST
MESH = pl.DeviceIdType.MESH
F32 = jnp.float32
BF16 = jnp.bfloat16

SHARDS = 8
PER = 5
NF = 80
VMEM_LIMIT = 60 * 1024 * 1024


def first_needed(shard):
    return max(2 * shard * PER - 1, 0)


def row_start(shard):
    return first_needed(shard) // 16 * 16


def sent_start(shard):
    return first_needed(shard) // 8 * 8

PHASES = (((0, 4, 5, 6, 7), (4, 5, 6, 7)), ((1, 2, 3), (0, 1, 2, 3)))
ORDER = (4, 3, 5, 2, 6, 1, 7)
KINDS = 8
EARLY = {0: (3, 4), 1: (), 2: (), 3: (5, 6, 7), 4: (5, 6, 7, 3, 4), 5: (5, 6, 7, 3, 4), 6: (5, 6, 7, 3, 4), 7: (3, 4)}
LATE = {0: (5, 6, 7), 1: (3, 4, 5, 6, 7), 2: (3, 4, 5, 6, 7), 3: (3, 4), 4: (), 5: (), 6: (), 7: ()}
GATE = ()


def halves(x):
    high = x.astype(BF16)
    low = (x - high.astype(F32)).astype(BF16)
    return high, low


def split_f32(x):
    high = x.astype(BF16).astype(F32)
    return high, (x - high).astype(BF16).astype(F32)


def zeros_above(top, x):
    if top == 0:
        return x
    return jnp.concatenate([jnp.zeros((top, x.shape[1]), x.dtype), x], axis=0)


class Scratch:
    pass


def constants(c, loads, curve):
    lane = lax.broadcasted_iota(jnp.int32, (128, 128), 1)
    row = lax.broadcasted_iota(jnp.int32, (128, 128), 0)
    c.square[...] = jnp.zeros((128, 128), F32)
    raw = loads[...]
    c.square[0:4, 0:NF] = raw / jnp.sqrt(jnp.sum(raw * raw, axis=0, keepdims=True))
    padded = c.square[...]
    turned = jnp.transpose(padded)
    full = jnp.dot(turned, padded, precision=HIGHEST, preferred_element_type=F32)
    part_high, part_low = split_f32(padded)

    high, low = split_f32(jnp.where(row <= lane, full, 0.0))
    c.stack[...] = jnp.zeros((256, 128), F32)
    c.stack[0:NF, :] = high[:NF]
    c.stack[NF : 2 * NF, :] = high[:NF]
    c.stack[2 * NF : 3 * NF, :] = low[:NF]
    c.stack[240:244, :] = part_high[0:4]
    c.stack[244:248, :] = part_high[0:4]
    c.stack[248:252, :] = part_low[0:4]
    c.forward_lhs[...] = jnp.transpose(c.stack[...])[:NF].astype(BF16)

    high, low = split_f32(jnp.where(row >= lane, full, 0.0))
    c.stack[...] = jnp.zeros((256, 128), F32)
    c.stack[0:NF, :] = high[:NF]
    c.stack[NF : 2 * NF, :] = low[:NF]
    c.backward_lhs[...] = jnp.transpose(c.stack[...])[:NF].astype(BF16)

    lower = jnp.where((row <= lane) & (row < NF), 1.0, 0.0)
    c.stack[0:NF, :] = lower[:NF]
    c.stack[NF : 2 * NF, :] = lower[:NF]
    c.sums_lhs[...] = jnp.transpose(c.stack[...])[:NF].astype(BF16)
    upper = jnp.where((row >= lane) & (row < NF), 1.0, 0.0)
    c.stack[0:NF, :] = upper[:NF]
    c.stack[NF : 2 * NF, :] = upper[:NF]
    c.tails_lhs[...] = jnp.transpose(c.stack[...])[:NF].astype(BF16)

    c.square[...] = jnp.zeros((128, 128), F32)
    c.square[0:1, 0:NF] = curve[...]
    column = jnp.transpose(c.square[...])[:NF, 0:1]
    c.start[0][...] = jnp.broadcast_to(column, (NF, c.width))


def tables(c):
    lane = lax.broadcasted_iota(jnp.int32, (SHARDS, 128), 1)
    row = lax.broadcasted_iota(jnp.int32, (128, 128), 0)
    c.square[...] = jnp.zeros((128, 128), F32)
    for s in range(SHARDS):
        c.square[s * PER : (s + 1) * PER, 0:NF] = c.vols[s]
    turned = jnp.transpose(c.square[...])
    for s in range(SHARDS):
        top = row_start(s)
        for k in range(PER):
            d = s * PER + k
            column = jnp.broadcast_to(turned[top:NF, d : d + 1], (NF - top, 128))
            c.sigma[s, k, top:NF, :] = jnp.where(row[top:NF] >= 2 * d + 1, column, 0.0)
    c.square[...] = jnp.zeros((128, 128), F32)
    for s in range(SHARDS):
        c.square[s * PER : (s + 1) * PER, 0:6] = c.regress[s]
    ids = jnp.concatenate([c.slots[s] for s in range(SHARDS)], axis=0)
    hot = jnp.concatenate(
        [
            jnp.where(jnp.broadcast_to(ids[:, k : k + 1], (SHARDS, 128)) == lane, 1.0, 0.0)
            for k in range(PER)
        ],
        axis=0,
    )
    c.weights[...] = jnp.dot(hot, c.square[...], precision=HIGHEST, preferred_element_type=F32)


def flag_rows(c, shards):
    for s in shards:
        for k in range(PER):
            c.flags[k, s : s + 1, :] = c.bits[s, k : k + 1, :].astype(F32)


def forward_pass(c, shards):
    a, width = ACCRUAL, c.width

    def wide(x):
        return jnp.concatenate([x] * (width // 128), axis=1)

    for s in shards:
        top = row_start(s)
        if s > 0:
            position = lax.broadcasted_iota(jnp.int32, (NF - top, width), 0) + top
            c.start[s][top:NF, :] = jnp.where(
                position >= first_needed(s), c.rates[s - 1, top:NF, :], STRIKE
            )
        c.state[s][top:NF, :] = c.start[s][top:NF, :]

    def drift(s, k, held):
        top = row_start(s)
        if s == 0:
            h = jnp.where(k == 0, a, 2.0 * a).astype(F32)
            root = jnp.where(k == 0, a**0.5, (2.0 * a) ** 0.5).astype(F32)
        else:
            h, root = 2.0 * a, (2.0 * a) ** 0.5
        current = c.state[s][top:NF, :]
        opening = 2 * (s * PER + k)
        second = 1.0 + a * c.state[s][pl.ds(opening, 1), :]
        if s == 0:
            before = 1.0 + a * c.state[s][pl.ds(jnp.maximum(opening - 1, 0), 1), :]
            before = jnp.where(k == 0, 1.0, before)
        else:
            before = 1.0 + a * c.state[s][pl.ds(opening - 1, 1), :]
        c.growth[k, s : s + 1, :] = before * second
        scaled = a * current
        v = scaled / (1.0 + scaled)
        c.v[s][k, top:NF, :] = v
        sig = wide(c.sigma[s, k, top:NF, :])
        hsig = h * sig
        high, low = halves(hsig * v)
        shock = root * c.shocks[s, k]
        shock_high = shock.astype(BF16).astype(F32)
        noise = jnp.concatenate(
            [shock_high, shock - shock_high, shock_high, jnp.zeros_like(shock)], axis=0
        ).astype(BF16)
        high, low = zeros_above(top, high), zeros_above(top, low)
        rhs = jnp.concatenate([high, low, high, noise], axis=0)
        w = jnp.dot(c.forward_lhs[top:NF, :], rhs, preferred_element_type=F32)
        held[s] = (w, sig, hsig, current)

    def moved(s, k, held):
        top = row_start(s)
        w, sig, hsig, current = held[s]
        c.w[s][k, top:NF, :] = w - hsig
        current = current * jnp.exp(sig * (w - 0.5 * hsig))
        c.state[s][top:NF, :] = current
        position = lax.broadcasted_iota(jnp.int32, (NF - top, width), 0) + top
        living = position > 2 * (s * PER + k)
        logs = jnp.where(living, jnp.log(1.0 + a * current), 0.0)
        high, low = halves(logs)
        rhs = jnp.concatenate([zeros_above(top, high), zeros_above(top, low)], axis=0)
        total = jnp.dot(c.sums_lhs[top:NF, 0 : 2 * NF], rhs, preferred_element_type=F32)
        held[s] = (total, living)

    def bonds_of(s, k, held):
        top = row_start(s)
        total, living = held[s]
        bonds = jnp.where(living, jnp.exp(-total), 0.0)
        c.annuity[k, s : s + 1, :] = a * jnp.sum(bonds, axis=0, keepdims=True)
        c.last[k, s : s + 1, :] = bonds[NF - top - 1 : NF - top]
        high, low = halves(bonds)
        rhs = jnp.concatenate([zeros_above(top, high), zeros_above(top, low)], axis=0)
        c.tail[s][k, top:NF, :] = jnp.dot(
            c.tails_lhs[top:NF, 0 : 2 * NF], rhs, preferred_element_type=F32
        )

    def forward(k, carry):
        held = {}
        count = len(shards)
        for step in range(count + 2):
            if step >= 2:
                bonds_of(shards[step - 2], k, held)
            if 1 <= step <= count:
                moved(shards[step - 1], k, held)
            if step < count:
                drift(shards[step], k, held)
        return carry

    lax.fori_loop(0, PER, forward, 0, unroll=True)
    for s in shards:
        top = row_start(s)
        scaled = a * c.state[s][top:NF, :]
        c.v[s][PER, top:NF, :] = scaled / (1.0 + scaled)


def exercise_pass(c, shards, s_now, n_now):
    a, width = ACCRUAL, c.width
    low, count = shards[0], len(shards)
    rows = slice(low, low + count)

    def starts(ref):
        lines = [ref[s - 1] if s > 0 else jnp.ones((1, width), F32) for s in shards]
        return jnp.concatenate(lines, axis=0)

    numeraire, survival = starts(c.numer), starts(c.survive)
    scale = c.path_weight * NOTIONAL
    kept = []
    values = jnp.zeros((count, width), F32)
    for k in range(PER):
        growth = c.growth[k, rows, :]
        numeraire = numeraire * growth
        annuity = c.annuity[k, rows, :]
        last = c.last[k, rows, :]
        floating = 1.0 - last
        exercise = floating - STRIKE * annuity
        inverse = 1.0 / annuity
        money = (floating * inverse - STRIKE) / SMOOTHING
        w = [
            jnp.broadcast_to(
                c.weights[k * SHARDS + low : k * SHARDS + low + count, b : b + 1], (count, width)
            )
            for b in range(6)
        ]
        slope = w[3] + money * (w[4] + money * w[5])
        continuation = w[0] + money * (w[1] + money * w[2]) + annuity * slope
        gate = 1.0 / (1.0 + jnp.exp(-(exercise - continuation) / SMOOTHING))
        chance = c.flags[k, rows, :] * gate
        discount = 1.0 / numeraire
        paid = exercise * discount
        values = values + NOTIONAL * survival * chance * paid
        kept.append(
            dict(
                numeraire=numeraire, survival=survival, floating=floating, growth=growth,
                last=last, inverse=inverse, slope=slope, gate=gate, chance=chance,
                discount=discount, paid=paid,
                d_money=w[1] + 2.0 * money * w[2] + annuity * (w[4] + 2.0 * money * w[5]),
            )
        )
        survival = survival * (1.0 - chance)

    one, zero = jnp.ones((count, width), F32), jnp.zeros((count, width), F32)
    s_mul, s_add, n_mul, n_add = one, zero, one, zero
    for k in reversed(range(PER)):
        e = kept[k]
        left = 1.0 - e["chance"]
        gain = scale * e["chance"] * e["paid"]
        s_mul, s_add = s_mul * left, s_add * left + gain
        e["n_push"] = -e["survival"] * gain * e["discount"]
        n_mul, n_add = n_mul * e["growth"], (n_add + e["n_push"]) * e["growth"]
    survive_end, numer_end = [None] * count, [None] * count
    for i in reversed(range(count)):
        survive_end[i], numer_end[i] = s_now, n_now
        s_now = s_mul[i : i + 1] * s_now + s_add[i : i + 1]
        n_now = n_mul[i : i + 1] * n_now + n_add[i : i + 1]
    d_survive = jnp.concatenate(survive_end, axis=0)
    d_numer = jnp.concatenate(numer_end, axis=0)
    for k in reversed(range(PER)):
        e = kept[k]
        d_numer = d_numer + e["n_push"]
        c.mult_numer[k, rows, :] = d_numer * e["numeraire"]
        d_numer = d_numer * e["growth"]
        d_chance = e["survival"] * (scale * e["paid"] - d_survive)
        d_score = d_chance * e["chance"] * (1.0 - e["gate"]) / SMOOTHING
        d_exercise = scale * e["survival"] * e["chance"] * e["discount"] + d_score
        d_money = -d_score * e["d_money"] / SMOOTHING
        ratio = d_money * e["inverse"]
        d_annuity = -d_score * e["slope"] - STRIKE * d_exercise - ratio * e["floating"] * e["inverse"]
        d_floating = d_exercise + ratio
        c.mult_tail[k, rows, :] = -a * d_annuity
        c.mult_last[k, rows, :] = d_floating * e["last"]
        d_survive = d_survive * (1.0 - e["chance"]) + scale * e["chance"] * e["paid"]
    return s_now, n_now, jnp.sum(values, axis=0, keepdims=True)


def backward_shard(c, s, pull):
    a, width = ACCRUAL, c.width
    top = row_start(s)
    count = NF - top
    position = lax.broadcasted_iota(jnp.int32, (count, width), 0) + top
    if s < SHARDS - 1:
        below = row_start(s + 1)
        ratio = c.state[s][below:NF, :] / c.start[s + 1][below:NF, :]
        pull = zeros_above(below - top, pull * ratio)

    def backward(step, pull):
        k = PER - 1 - step
        opening = 2 * (s * PER + k)
        h = 2.0 * a
        if s == 0:
            h = jnp.where(k == 0, a, 2.0 * a).astype(F32)
        narrow = c.sigma[s, k, top:NF, :]
        sig = jnp.concatenate([narrow] * (width // 128), axis=1)
        v = c.v[s][k, top:NF, :]
        push = c.mult_last[k, s : s + 1, :] + c.mult_tail[k, s : s + 1, :] * c.tail[s][k, top:NF, :]
        y = pull + jnp.where(position > opening, c.v[s][k + 1, top:NF, :] * push, 0.0)
        part = zeros_above(top, (h * sig * y).astype(BF16))
        rhs = jnp.concatenate([part, part], axis=0)
        du = jnp.dot(c.backward_lhs[top:NF, 0 : 2 * NF], rhs, preferred_element_type=F32)
        fixed = (position == opening) | (position == opening - 1)
        base = y + jnp.where(fixed, v * c.mult_numer[k, s : s + 1, :], 0.0)
        factor = sig * (v * (1.0 - v))
        out = base + factor * du
        by_vol = jnp.where(position > opening, y * c.w[s][k, top:NF, :] + du * v, 0.0)
        folded = by_vol[:, 0:128]
        for piece in range(1, width // 128):
            folded = folded + by_vol[:, piece * 128 : (piece + 1) * 128]
        c.by_vol[s][k, top:NF, :] = folded
        return out

    return lax.fori_loop(0, PER, backward, pull, unroll=True)


def sum_paths(c, shards):
    for s in shards:
        top = row_start(s)
        lanes = lax.broadcasted_iota(jnp.int32, (NF - top, 128), 1)
        gathered = c.square[top:NF, :]
        for k in range(PER):
            summed = jnp.sum(c.by_vol[s][k, top:NF, :], axis=1, keepdims=True)
            gathered = jnp.where(lanes == s * PER + k, summed, gathered)
        c.square[top:NF, :] = gathered


def kernel(
    path_weight, groups,
    curve, loads, shocks, bits, rates, numer, survive, vols, regress, slots,
    vega, values,
    shocks_x, bits_x, rates_x, numer_x, survive_x, vols_x, regress_x, slots_x,
    square, stack, forward_lhs, backward_lhs, sums_lhs, tails_lhs, sigma, weights,
    growth, annuity, last, flags, mult_tail, mult_last, mult_numer,
    part, landed, value, values_landed, summed, spread,
    *rest,
):
    per_shard, sems = rest[: 6 * SHARDS], rest[6 * SHARDS :]
    (send_sem, recv_sem, local_sem, part_send, part_recv, value_send, value_recv,
     spread_send, spread_recv) = sems
    c = Scratch()
    c.path_weight, c.width = path_weight, shocks_x.shape[3]
    c.shocks, c.bits, c.rates, c.numer, c.survive = shocks_x, bits_x, rates_x, numer_x, survive_x
    c.vols, c.regress, c.slots = vols_x, regress_x, slots_x
    c.square, c.stack, c.sigma, c.weights = square, stack, sigma, weights
    c.forward_lhs, c.backward_lhs = forward_lhs, backward_lhs
    c.sums_lhs, c.tails_lhs = sums_lhs, tails_lhs
    c.growth, c.annuity, c.last, c.flags = growth, annuity, last, flags
    c.mult_tail, c.mult_last, c.mult_numer = mult_tail, mult_last, mult_numer
    c.state, c.start, c.v, c.w, c.tail, c.by_vol = (
        per_shard[i * SHARDS : (i + 1) * SHARDS] for i in range(6)
    )
    width = c.width
    me = lax.axis_index("tm")
    group = lax.axis_index("paths")

    barrier = pltpu.get_barrier_semaphore()
    for step in ORDER:
        other = lax.rem(me + step, SHARDS)
        pl.semaphore_signal(barrier, inc=1, device_id={"tm": other}, device_id_type=MESH)
    for step in range(1, groups):
        other = lax.rem(group + step, groups)
        pl.semaphore_signal(barrier, inc=1, device_id={"paths": other}, device_id_type=MESH)

    def cut(target):
        return pl.ds(pl.multiple_of(target * width, width), width)

    def pair_of(kind, source, target):
        if kind == 0:
            return vols, vols_x.at[source]
        if kind == 1:
            return regress, regress_x.at[source]
        if kind == 2:
            return slots, slots_x.at[source]
        if kind == 3:
            return shocks.at[:, :, cut(target)], shocks_x.at[source]
        if kind == 4:
            return bits.at[:, cut(target)], bits_x.at[source]
        if kind == 5:
            return numer.at[:, cut(target)], numer_x.at[source]
        if kind == 6:
            return survive.at[:, cut(target)], survive_x.at[source]
        top = sent_start(source + 1)
        rows = pl.ds(top, NF - top)
        return rates.at[0, rows, cut(target)], rates_x.at[source, rows, :]

    def here(kind, source):
        src, dst = pair_of(kind, source, source)
        return pltpu.make_async_copy(src, dst, local_sem.at[kind])

    def remote(kind, source, step, target):
        src, dst = pair_of(kind, source, target)
        return pltpu.make_async_remote_copy(
            src_ref=src, dst_ref=dst,
            send_sem=send_sem.at[kind, step], recv_sem=recv_sem.at[kind, source],
            device_id={"tm": target}, device_id_type=MESH,
        )

    def by_source(plan, action):
        for source in everyone:
            if plan[source]:

                @pl.when(me == source)
                def _():
                    action(source, plan[source])

    def start_sends(source, kinds):
        for step in ORDER:
            for kind in kinds:
                remote(kind, source, step, lax.rem(me + step, SHARDS)).start()

    def end_sends(source, kinds):
        for step in ORDER:
            for kind in kinds:
                remote(kind, source, step, lax.rem(me + step, SHARDS)).wait_send()

    def start_here(source, kinds):
        for kind in kinds:
            here(kind, source).start()

    def await_kinds(kinds, sources):
        for source in sources:
            wanted = [kind for kind in kinds if (kind, source) not in seen]
            seen.update((kind, source) for kind in wanted)
            if not wanted:
                continue

            @pl.when(me != source)
            def _():
                for kind in wanted:
                    remote(kind, source, 0, source).wait_recv()

            @pl.when(me == source)
            def _():
                for kind in wanted:
                    here(kind, source).wait()

    everyone = range(SHARDS)
    seen = set()
    for kind in range(3):
        here(kind, me).start()
    by_source(EARLY, start_here)
    by_source(LATE, start_here)
    constants(c, loads, curve)
    pl.semaphore_wait(barrier, SHARDS - 1 + groups - 1)
    start_sends(me, (0, 1, 2))
    by_source(EARLY, start_sends)
    await_kinds((0, 1, 2), everyone)
    for kinds, source in GATE:
        await_kinds(kinds, (source,))
    by_source(LATE, start_sends)
    tables(c)

    s_now = jnp.zeros((1, width), F32)
    n_now = jnp.zeros((1, width), F32)
    pull = jnp.zeros((NF - row_start(SHARDS - 1), width), F32)
    paid = None
    flagged = set()
    square[...] = jnp.zeros((128, 128), F32)
    for first_shards, shards in PHASES:
        fresh = [s for s in dict.fromkeys(first_shards + shards) if s not in flagged]
        flagged.update(fresh)
        await_kinds((3, 4), fresh)
        flag_rows(c, fresh)
        await_kinds((5, 6, 7), [s - 1 for s in reversed(fresh) if s > 0])
        forward_pass(c, first_shards)
        s_now, n_now, gains = exercise_pass(c, shards, s_now, n_now)
        paid = gains if paid is None else paid + gains
        if shards[0] == 0:
            value[...] = paid
        for s in reversed(shards):
            pull = backward_shard(c, s, pull)
        sum_paths(c, shards)

    turned = jnp.transpose(square[...])
    for s in range(SHARDS):
        part[s] = turned[s * PER : (s + 1) * PER, :]

    def block(step, source, target):
        return pltpu.make_async_remote_copy(
            src_ref=part.at[target], dst_ref=landed.at[source],
            send_sem=part_send.at[step], recv_sem=part_recv.at[source],
            device_id={"tm": target}, device_id_type=MESH,
        )

    def line(step, source, target):
        return pltpu.make_async_remote_copy(
            src_ref=value, dst_ref=values_landed.at[source],
            send_sem=value_send.at[step], recv_sem=value_recv.at[source],
            device_id={"tm": target}, device_id_type=MESH,
        )

    def share(step, source, target):
        return pltpu.make_async_remote_copy(
            src_ref=summed, dst_ref=spread.at[source],
            send_sem=spread_send.at[step], recv_sem=spread_recv.at[source],
            device_id={"paths": target}, device_id_type=MESH,
        )

    for step in ORDER:
        line(step, me, lax.rem(me + step, SHARDS)).start()
    for step in ORDER:
        block(step, me, lax.rem(me + step, SHARDS)).start()
    landed[me] = part[me]
    values_landed[me] = value[...]
    end_sends(me, (0, 1, 2))
    by_source(EARLY, end_sends)
    by_source(LATE, end_sends)
    for source in everyone:

        @pl.when(me != source)
        def _():
            block(0, source, source).wait_recv()

    total = landed[0]
    for source in range(1, SHARDS):
        total = total + landed[source]
    summed[...] = total
    spread[group] = total
    for source in everyone:

        @pl.when(me != source)
        def _():
            line(0, source, source).wait_recv()

    for step in range(1, groups):
        share(step, group, lax.rem(group + step, groups)).start()
    for source in everyone:
        values[0:1, source * width : (source + 1) * width] = values_landed[source]
    for step in ORDER:
        block(step, me, lax.rem(me + step, SHARDS)).wait_send()
        line(step, me, lax.rem(me + step, SHARDS)).wait_send()
    for step in range(1, groups):
        share(step, group, lax.rem(group + step, groups)).wait_send()
    for step in range(1, groups):
        source = lax.rem(group + step, groups)
        share(0, source, source).wait_recv()
    total = spread[0]
    for source in range(1, groups):
        total = total + spread[source]
    vega[...] = total[:, 0:NF]


def local(
    start_curve, loadings, vols, shocks, exercise_bits, regress, date_slot,
    ck_rates, ck_numer, ck_survive,
):
    groups = lax.axis_size("paths")
    path_count = shocks.shape[2]
    width = path_count // SHARDS
    inside = pl.BlockSpec(memory_space=pltpu.VMEM)
    anywhere = pl.BlockSpec(memory_space=pl.ANY)
    small = pltpu.VMEM((PER, SHARDS, width), F32)
    lhs = pltpu.VMEM((NF, 256), BF16)
    plane = pltpu.VMEM((NF, width), F32)
    dates = pltpu.VMEM((PER, NF, width), F32)
    dma = pltpu.SemaphoreType.DMA
    vega, values = pl.pallas_call(
        functools.partial(kernel, NOTIONAL / (path_count * groups), groups),
        name="pathwise_vega",
        out_shape=[
            jax.ShapeDtypeStruct((PER, NF), F32),
            jax.ShapeDtypeStruct((1, path_count), F32),
        ],
        in_specs=[inside] * 2 + [anywhere] * 8,
        out_specs=[inside] * 2,
        scratch_shapes=[
            pltpu.VMEM((SHARDS, PER, 4, width), F32),
            pltpu.VMEM((SHARDS, PER, width), jnp.int32),
            pltpu.VMEM((SHARDS, NF, width), F32),
            pltpu.VMEM((SHARDS, 1, width), F32),
            pltpu.VMEM((SHARDS, 1, width), F32),
            pltpu.VMEM((SHARDS, PER, NF), F32),
            pltpu.VMEM((SHARDS, PER, 6), F32),
            pltpu.VMEM((SHARDS, 1, PER), jnp.int32),
            pltpu.VMEM((128, 128), F32),
            pltpu.VMEM((256, 128), F32),
            lhs, lhs, lhs, lhs,
            pltpu.VMEM((SHARDS, PER, NF, 128), F32),
            pltpu.VMEM((PER * SHARDS, 128), F32),
            small, small, small, small,
            small, small, small,
            pltpu.VMEM((SHARDS, PER, 128), F32),
            pltpu.VMEM((SHARDS, PER, 128), F32),
            pltpu.VMEM((1, width), F32),
            pltpu.VMEM((SHARDS, 1, width), F32),
            pltpu.VMEM((PER, 128), F32),
            pltpu.VMEM((groups, PER, 128), F32),
        ]
        + [plane] * SHARDS
        + [plane] * SHARDS
        + [pltpu.VMEM((PER + 1, NF, width), F32)] * SHARDS
        + [dates] * SHARDS
        + [dates] * SHARDS
        + [pltpu.VMEM((PER, NF, 128), F32)] * SHARDS
        + [
            dma((KINDS, SHARDS)), dma((KINDS, SHARDS)), dma((KINDS,)),
            dma((SHARDS,)), dma((SHARDS,)), dma((SHARDS,)), dma((SHARDS,)),
            dma((groups,)), dma((groups,)),
        ],
        compiler_params=pltpu.CompilerParams(
            collective_id=0, has_side_effects=True, vmem_limit_bytes=VMEM_LIMIT
        ),
    )(
        start_curve.reshape(1, NF), loadings, shocks, exercise_bits, ck_rates, ck_numer,
        ck_survive, vols, regress, date_slot.reshape(1, PER),
    )
    return (vega, values.reshape(path_count))


def solution(mesh):
    return jax.shard_map(
        local,
        mesh=mesh,
        in_specs=(
            P(),
            P(),
            P("tm", None),
            P("tm", None, "paths"),
            P("tm", "paths"),
            P("tm", None),
            P("tm"),
            P("tm", None, "paths"),
            P("tm", "paths"),
            P("tm", "paths"),
        ),
        out_specs=(P("tm", None), P("paths")),
        check_vma=False,
    )
```

```python
import functools

import jax
import jax.numpy as jnp
from jax import lax
from jax.experimental import pallas as pl
from jax.experimental.pallas import tpu as pltpu
from jax.sharding import PartitionSpec as P

ACCRUAL = 0.25
STRIKE = 0.04
SMOOTHING = 0.01
NOTIONAL = 100.0
HIGHEST = lax.Precision.HIGHEST
MESH = pl.DeviceIdType.MESH
F32 = jnp.float32
BF16 = jnp.bfloat16

SHARDS = 8
PER = 5
NF = 80
VMEM_LIMIT = 60 * 1024 * 1024


def first_needed(shard):
    return max(2 * shard * PER - 1, 0)


def row_start(shard):
    return first_needed(shard) // 16 * 16


def sent_start(shard):
    return first_needed(shard) // 8 * 8

PHASES = (((0, 4, 5, 6, 7), (4, 5, 6, 7)), ((1, 2, 3), (0, 1, 2, 3)))
ORDER = (4, 3, 5, 2, 6, 1, 7)
KINDS = 8
EARLY = {0: (3, 4), 1: (), 2: (), 3: (5, 6, 7), 4: (5, 6, 7, 3, 4), 5: (5, 6, 7, 3, 4), 6: (5, 6, 7, 3, 4), 7: (3, 4)}
LATE = {0: (5, 6, 7), 1: (3, 4, 5, 6, 7), 2: (3, 4, 5, 6, 7), 3: (3, 4), 4: (), 5: (), 6: (), 7: ()}


def halves(x):
    high = x.astype(BF16)
    low = (x - high.astype(F32)).astype(BF16)
    return high, low


def split_f32(x):
    high = x.astype(BF16).astype(F32)
    return high, (x - high).astype(BF16).astype(F32)


def zeros_above(top, x):
    if top == 0:
        return x
    return jnp.concatenate([jnp.zeros((top, x.shape[1]), x.dtype), x], axis=0)


class Scratch:
    pass


def constants(c, loads, curve):
    lane = lax.broadcasted_iota(jnp.int32, (128, 128), 1)
    row = lax.broadcasted_iota(jnp.int32, (128, 128), 0)
    c.square[...] = jnp.zeros((128, 128), F32)
    raw = loads[...]
    c.square[0:4, 0:NF] = raw / jnp.sqrt(jnp.sum(raw * raw, axis=0, keepdims=True))
    padded = c.square[...]
    turned = jnp.transpose(padded)
    full = jnp.dot(turned, padded, precision=HIGHEST, preferred_element_type=F32)
    part_high, part_low = split_f32(padded)

    high, low = split_f32(jnp.where(row <= lane, full, 0.0))
    c.stack[...] = jnp.zeros((256, 128), F32)
    c.stack[0:NF, :] = high[:NF]
    c.stack[NF : 2 * NF, :] = high[:NF]
    c.stack[2 * NF : 3 * NF, :] = low[:NF]
    c.stack[240:244, :] = part_high[0:4]
    c.stack[244:248, :] = part_high[0:4]
    c.stack[248:252, :] = part_low[0:4]
    c.forward_lhs[...] = jnp.transpose(c.stack[...])[:NF].astype(BF16)

    high, low = split_f32(jnp.where(row >= lane, full, 0.0))
    c.stack[...] = jnp.zeros((256, 128), F32)
    c.stack[0:NF, :] = high[:NF]
    c.stack[NF : 2 * NF, :] = low[:NF]
    c.backward_lhs[...] = jnp.transpose(c.stack[...])[:NF].astype(BF16)

    lower = jnp.where((row <= lane) & (row < NF), 1.0, 0.0)
    c.stack[0:NF, :] = lower[:NF]
    c.stack[NF : 2 * NF, :] = lower[:NF]
    c.sums_lhs[...] = jnp.transpose(c.stack[...])[:NF].astype(BF16)
    upper = jnp.where((row >= lane) & (row < NF), 1.0, 0.0)
    c.stack[0:NF, :] = upper[:NF]
    c.stack[NF : 2 * NF, :] = upper[:NF]
    c.tails_lhs[...] = jnp.transpose(c.stack[...])[:NF].astype(BF16)

    c.square[...] = jnp.zeros((128, 128), F32)
    c.square[0:1, 0:NF] = curve[...]
    column = jnp.transpose(c.square[...])[:NF, 0:1]
    c.start[0][...] = jnp.broadcast_to(column, (NF, c.width))


def tables(c):
    lane = lax.broadcasted_iota(jnp.int32, (SHARDS, 128), 1)
    row = lax.broadcasted_iota(jnp.int32, (128, 128), 0)
    c.square[...] = jnp.zeros((128, 128), F32)
    for s in range(SHARDS):
        c.square[s * PER : (s + 1) * PER, 0:NF] = c.vols[s]
    turned = jnp.transpose(c.square[...])
    for s in range(SHARDS):
        top = row_start(s)
        for k in range(PER):
            d = s * PER + k
            column = jnp.broadcast_to(turned[top:NF, d : d + 1], (NF - top, 128))
            c.sigma[s, k, top:NF, :] = jnp.where(row[top:NF] >= 2 * d + 1, column, 0.0)
    c.square[...] = jnp.zeros((128, 128), F32)
    for s in range(SHARDS):
        c.square[s * PER : (s + 1) * PER, 0:6] = c.regress[s]
    ids = jnp.concatenate([c.slots[s] for s in range(SHARDS)], axis=0)
    hot = jnp.concatenate(
        [
            jnp.where(jnp.broadcast_to(ids[:, k : k + 1], (SHARDS, 128)) == lane, 1.0, 0.0)
            for k in range(PER)
        ],
        axis=0,
    )
    c.weights[...] = jnp.dot(hot, c.square[...], precision=HIGHEST, preferred_element_type=F32)


def flag_rows(c, shards):
    for s in shards:
        for k in range(PER):
            c.flags[k, s : s + 1, :] = c.bits[s, k : k + 1, :].astype(F32)


def forward_pass(c, shards):
    a, width = ACCRUAL, c.width

    def wide(x):
        return jnp.concatenate([x] * (width // 128), axis=1)

    for s in shards:
        top = row_start(s)
        if s > 0:
            position = lax.broadcasted_iota(jnp.int32, (NF - top, width), 0) + top
            c.start[s][top:NF, :] = jnp.where(
                position >= first_needed(s), c.rates[s - 1, top:NF, :], STRIKE
            )
        c.state[s][top:NF, :] = c.start[s][top:NF, :]

    def drift(s, k, held):
        top = row_start(s)
        if s == 0:
            h = jnp.where(k == 0, a, 2.0 * a).astype(F32)
            root = jnp.where(k == 0, a**0.5, (2.0 * a) ** 0.5).astype(F32)
        else:
            h, root = 2.0 * a, (2.0 * a) ** 0.5
        current = c.state[s][top:NF, :]
        opening = 2 * (s * PER + k)
        second = 1.0 + a * c.state[s][pl.ds(opening, 1), :]
        if s == 0:
            before = 1.0 + a * c.state[s][pl.ds(jnp.maximum(opening - 1, 0), 1), :]
            before = jnp.where(k == 0, 1.0, before)
        else:
            before = 1.0 + a * c.state[s][pl.ds(opening - 1, 1), :]
        c.growth[k, s : s + 1, :] = before * second
        scaled = a * current
        v = scaled / (1.0 + scaled)
        c.v[s][k, top:NF, :] = v
        sig = wide(c.sigma[s, k, top:NF, :])
        hsig = h * sig
        high, low = halves(hsig * v)
        shock = root * c.shocks[s, k]
        shock_high = shock.astype(BF16).astype(F32)
        noise = jnp.concatenate(
            [shock_high, shock - shock_high, shock_high, jnp.zeros_like(shock)], axis=0
        ).astype(BF16)
        high, low = zeros_above(top, high), zeros_above(top, low)
        rhs = jnp.concatenate([high, low, high, noise], axis=0)
        w = jnp.dot(c.forward_lhs[top:NF, :], rhs, preferred_element_type=F32)
        held[s] = (w, sig, hsig, current)

    def moved(s, k, held):
        top = row_start(s)
        w, sig, hsig, current = held[s]
        c.w[s][k, top:NF, :] = w - hsig
        current = current * jnp.exp(sig * (w - 0.5 * hsig))
        c.state[s][top:NF, :] = current
        position = lax.broadcasted_iota(jnp.int32, (NF - top, width), 0) + top
        living = position > 2 * (s * PER + k)
        logs = jnp.where(living, jnp.log(1.0 + a * current), 0.0)
        high, low = halves(logs)
        rhs = jnp.concatenate([zeros_above(top, high), zeros_above(top, low)], axis=0)
        total = jnp.dot(c.sums_lhs[top:NF, 0 : 2 * NF], rhs, preferred_element_type=F32)
        held[s] = (total, living)

    def bonds_of(s, k, held):
        top = row_start(s)
        total, living = held[s]
        bonds = jnp.where(living, jnp.exp(-total), 0.0)
        c.annuity[k, s : s + 1, :] = a * jnp.sum(bonds, axis=0, keepdims=True)
        c.last[k, s : s + 1, :] = bonds[NF - top - 1 : NF - top]
        high, low = halves(bonds)
        rhs = jnp.concatenate([zeros_above(top, high), zeros_above(top, low)], axis=0)
        c.tail[s][k, top:NF, :] = jnp.dot(
            c.tails_lhs[top:NF, 0 : 2 * NF], rhs, preferred_element_type=F32
        )

    def forward(k, carry):
        held = {}
        count = len(shards)
        for step in range(count + 2):
            if step >= 2:
                bonds_of(shards[step - 2], k, held)
            if 1 <= step <= count:
                moved(shards[step - 1], k, held)
            if step < count:
                drift(shards[step], k, held)
        return carry

    lax.fori_loop(0, PER, forward, 0, unroll=True)
    for s in shards:
        top = row_start(s)
        scaled = a * c.state[s][top:NF, :]
        c.v[s][PER, top:NF, :] = scaled / (1.0 + scaled)


def exercise_pass(c, shards, s_now, n_now):
    a, width = ACCRUAL, c.width
    low, count = shards[0], len(shards)
    rows = slice(low, low + count)

    def starts(ref):
        lines = [ref[s - 1] if s > 0 else jnp.ones((1, width), F32) for s in shards]
        return jnp.concatenate(lines, axis=0)

    numeraire, survival = starts(c.numer), starts(c.survive)
    scale = c.path_weight * NOTIONAL
    kept = []
    values = jnp.zeros((count, width), F32)
    for k in range(PER):
        growth = c.growth[k, rows, :]
        numeraire = numeraire * growth
        annuity = c.annuity[k, rows, :]
        last = c.last[k, rows, :]
        floating = 1.0 - last
        exercise = floating - STRIKE * annuity
        inverse = 1.0 / annuity
        money = (floating * inverse - STRIKE) / SMOOTHING
        w = [
            jnp.broadcast_to(
                c.weights[k * SHARDS + low : k * SHARDS + low + count, b : b + 1], (count, width)
            )
            for b in range(6)
        ]
        slope = w[3] + money * (w[4] + money * w[5])
        continuation = w[0] + money * (w[1] + money * w[2]) + annuity * slope
        gate = 1.0 / (1.0 + jnp.exp(-(exercise - continuation) / SMOOTHING))
        chance = c.flags[k, rows, :] * gate
        discount = 1.0 / numeraire
        paid = exercise * discount
        values = values + NOTIONAL * survival * chance * paid
        kept.append(
            dict(
                numeraire=numeraire, survival=survival, floating=floating, growth=growth,
                last=last, inverse=inverse, slope=slope, gate=gate, chance=chance,
                discount=discount, paid=paid,
                d_money=w[1] + 2.0 * money * w[2] + annuity * (w[4] + 2.0 * money * w[5]),
            )
        )
        survival = survival * (1.0 - chance)

    one, zero = jnp.ones((count, width), F32), jnp.zeros((count, width), F32)
    s_mul, s_add, n_mul, n_add = one, zero, one, zero
    for k in reversed(range(PER)):
        e = kept[k]
        left = 1.0 - e["chance"]
        gain = scale * e["chance"] * e["paid"]
        s_mul, s_add = s_mul * left, s_add * left + gain
        e["n_push"] = -e["survival"] * gain * e["discount"]
        n_mul, n_add = n_mul * e["growth"], (n_add + e["n_push"]) * e["growth"]
    survive_end, numer_end = [None] * count, [None] * count
    for i in reversed(range(count)):
        survive_end[i], numer_end[i] = s_now, n_now
        s_now = s_mul[i : i + 1] * s_now + s_add[i : i + 1]
        n_now = n_mul[i : i + 1] * n_now + n_add[i : i + 1]
    d_survive = jnp.concatenate(survive_end, axis=0)
    d_numer = jnp.concatenate(numer_end, axis=0)
    for k in reversed(range(PER)):
        e = kept[k]
        d_numer = d_numer + e["n_push"]
        c.mult_numer[k, rows, :] = d_numer * e["numeraire"]
        d_numer = d_numer * e["growth"]
        d_chance = e["survival"] * (scale * e["paid"] - d_survive)
        d_score = d_chance * e["chance"] * (1.0 - e["gate"]) / SMOOTHING
        d_exercise = scale * e["survival"] * e["chance"] * e["discount"] + d_score
        d_money = -d_score * e["d_money"] / SMOOTHING
        ratio = d_money * e["inverse"]
        d_annuity = -d_score * e["slope"] - STRIKE * d_exercise - ratio * e["floating"] * e["inverse"]
        d_floating = d_exercise + ratio
        c.mult_tail[k, rows, :] = -a * d_annuity
        c.mult_last[k, rows, :] = d_floating * e["last"]
        d_survive = d_survive * (1.0 - e["chance"]) + scale * e["chance"] * e["paid"]
    return s_now, n_now, jnp.sum(values, axis=0, keepdims=True)


def backward_shard(c, s, pull):
    a, width = ACCRUAL, c.width
    top = row_start(s)
    count = NF - top
    position = lax.broadcasted_iota(jnp.int32, (count, width), 0) + top
    if s < SHARDS - 1:
        below = row_start(s + 1)
        ratio = c.state[s][below:NF, :] / c.start[s + 1][below:NF, :]
        pull = zeros_above(below - top, pull * ratio)

    def backward(step, pull):
        k = PER - 1 - step
        opening = 2 * (s * PER + k)
        h = 2.0 * a
        if s == 0:
            h = jnp.where(k == 0, a, 2.0 * a).astype(F32)
        narrow = c.sigma[s, k, top:NF, :]
        sig = jnp.concatenate([narrow] * (width // 128), axis=1)
        v = c.v[s][k, top:NF, :]
        push = c.mult_last[k, s : s + 1, :] + c.mult_tail[k, s : s + 1, :] * c.tail[s][k, top:NF, :]
        y = pull + jnp.where(position > opening, c.v[s][k + 1, top:NF, :] * push, 0.0)
        part = zeros_above(top, (h * sig * y).astype(BF16))
        rhs = jnp.concatenate([part, part], axis=0)
        du = jnp.dot(c.backward_lhs[top:NF, 0 : 2 * NF], rhs, preferred_element_type=F32)
        fixed = (position == opening) | (position == opening - 1)
        base = y + jnp.where(fixed, v * c.mult_numer[k, s : s + 1, :], 0.0)
        factor = sig * (v * (1.0 - v))
        out = base + factor * du
        by_vol = jnp.where(position > opening, y * c.w[s][k, top:NF, :] + du * v, 0.0)
        folded = by_vol[:, 0:128]
        for piece in range(1, width // 128):
            folded = folded + by_vol[:, piece * 128 : (piece + 1) * 128]
        c.by_vol[s][k, top:NF, :] = folded
        return out

    return lax.fori_loop(0, PER, backward, pull, unroll=True)


def sum_paths(c, shards):
    for s in shards:
        top = row_start(s)
        lanes = lax.broadcasted_iota(jnp.int32, (NF - top, 128), 1)
        gathered = c.square[top:NF, :]
        for k in range(PER):
            summed = jnp.sum(c.by_vol[s][k, top:NF, :], axis=1, keepdims=True)
            gathered = jnp.where(lanes == s * PER + k, summed, gathered)
        c.square[top:NF, :] = gathered


def kernel(
    path_weight, groups,
    curve_in, loads_in, shocks, bits, rates, numer, survive, vols, regress, slots,
    vega, values,
    curve, loads,
    shocks_x, bits_x, rates_x, numer_x, survive_x, vols_x, regress_x, slots_x,
    square, stack, forward_lhs, backward_lhs, sums_lhs, tails_lhs, sigma, weights,
    growth, annuity, last, flags, mult_tail, mult_last, mult_numer,
    part, landed, value, values_landed, summed, spread,
    *rest,
):
    per_shard, sems = rest[: 6 * SHARDS], rest[6 * SHARDS :]
    (send_sem, recv_sem, local_sem, part_send, part_recv, value_send, value_recv,
     spread_send, spread_recv) = sems
    c = Scratch()
    c.path_weight, c.width = path_weight, shocks_x.shape[3]
    c.shocks, c.bits, c.rates, c.numer, c.survive = shocks_x, bits_x, rates_x, numer_x, survive_x
    c.vols, c.regress, c.slots = vols_x, regress_x, slots_x
    c.square, c.stack, c.sigma, c.weights = square, stack, sigma, weights
    c.forward_lhs, c.backward_lhs = forward_lhs, backward_lhs
    c.sums_lhs, c.tails_lhs = sums_lhs, tails_lhs
    c.growth, c.annuity, c.last, c.flags = growth, annuity, last, flags
    c.mult_tail, c.mult_last, c.mult_numer = mult_tail, mult_last, mult_numer
    c.state, c.start, c.v, c.w, c.tail, c.by_vol = (
        per_shard[i * SHARDS : (i + 1) * SHARDS] for i in range(6)
    )
    width = c.width
    me = lax.axis_index("tm")
    group = lax.axis_index("paths")

    barrier = pltpu.get_barrier_semaphore()
    for step in ORDER:
        other = lax.rem(me + step, SHARDS)
        pl.semaphore_signal(barrier, inc=1, device_id={"tm": other}, device_id_type=MESH)
    for step in range(1, groups):
        other = lax.rem(group + step, groups)
        pl.semaphore_signal(barrier, inc=1, device_id={"paths": other}, device_id_type=MESH)

    def cut(target):
        return pl.ds(pl.multiple_of(target * width, width), width)

    def pair_of(kind, source, target):
        if kind == 0:
            return vols, vols_x.at[source]
        if kind == 1:
            return regress, regress_x.at[source]
        if kind == 2:
            return slots, slots_x.at[source]
        if kind == 3:
            return shocks.at[:, :, cut(target)], shocks_x.at[source]
        if kind == 4:
            return bits.at[:, cut(target)], bits_x.at[source]
        if kind == 5:
            return numer.at[:, cut(target)], numer_x.at[source]
        if kind == 6:
            return survive.at[:, cut(target)], survive_x.at[source]
        top = sent_start(source + 1)
        rows = pl.ds(top, NF - top)
        return rates.at[0, rows, cut(target)], rates_x.at[source, rows, :]

    def here(kind, source):
        src, dst = pair_of(kind, source, source)
        return pltpu.make_async_copy(src, dst, local_sem.at[kind])

    def remote(kind, source, step, target):
        src, dst = pair_of(kind, source, target)
        return pltpu.make_async_remote_copy(
            src_ref=src, dst_ref=dst,
            send_sem=send_sem.at[kind, step], recv_sem=recv_sem.at[kind, source],
            device_id={"tm": target}, device_id_type=MESH,
        )

    def by_source(plan, action):
        for source in everyone:
            if plan[source]:

                @pl.when(me == source)
                def _():
                    action(source, plan[source])

    def start_sends(source, kinds):
        for step in ORDER:
            for kind in kinds:
                remote(kind, source, step, lax.rem(me + step, SHARDS)).start()

    def end_sends(source, kinds):
        for step in ORDER:
            for kind in kinds:
                remote(kind, source, step, lax.rem(me + step, SHARDS)).wait_send()

    def start_here(source, kinds):
        for kind in kinds:
            here(kind, source).start()

    def await_kinds(kinds, sources):
        for source in sources:
            wanted = [kind for kind in kinds if (kind, source) not in seen]
            seen.update((kind, source) for kind in wanted)
            if not wanted:
                continue

            @pl.when(me != source)
            def _():
                for kind in wanted:
                    remote(kind, source, 0, source).wait_recv()

            @pl.when(me == source)
            def _():
                for kind in wanted:
                    here(kind, source).wait()

    everyone = range(SHARDS)
    seen = set()
    copies = [
        pltpu.make_async_copy(source, target, local_sem.at[KINDS + i])
        for i, (source, target) in enumerate(((curve_in, curve), (loads_in, loads)))
    ]
    for copy in copies:
        copy.start()
    pl.semaphore_wait(barrier, SHARDS - 1 + groups - 1)
    start_sends(me, (0, 1, 2))
    by_source(EARLY, start_sends)
    for kind in range(3):
        here(kind, me).start()
    by_source(EARLY, start_here)
    by_source(LATE, start_here)
    for copy in copies:
        copy.wait()
    constants(c, loads, curve)
    await_kinds((0, 1, 2), everyone)
    tables(c)
    by_source(LATE, start_sends)

    s_now = jnp.zeros((1, width), F32)
    n_now = jnp.zeros((1, width), F32)
    pull = jnp.zeros((NF - row_start(SHARDS - 1), width), F32)
    paid = None
    flagged = set()
    square[...] = jnp.zeros((128, 128), F32)
    for first_shards, shards in PHASES:
        fresh = [s for s in dict.fromkeys(first_shards + shards) if s not in flagged]
        flagged.update(fresh)
        await_kinds((3, 4), fresh)
        flag_rows(c, fresh)
        await_kinds((5, 6, 7), [s - 1 for s in reversed(fresh) if s > 0])
        forward_pass(c, first_shards)
        s_now, n_now, gains = exercise_pass(c, shards, s_now, n_now)
        paid = gains if paid is None else paid + gains
        if shards[0] == 0:
            value[...] = paid
        for s in reversed(shards):
            pull = backward_shard(c, s, pull)
        sum_paths(c, shards)

    turned = jnp.transpose(square[...])
    for s in range(SHARDS):
        part[s] = turned[s * PER : (s + 1) * PER, :]

    def block(step, source, target):
        return pltpu.make_async_remote_copy(
            src_ref=part.at[target], dst_ref=landed.at[source],
            send_sem=part_send.at[step], recv_sem=part_recv.at[source],
            device_id={"tm": target}, device_id_type=MESH,
        )

    def line(step, source, target):
        return pltpu.make_async_remote_copy(
            src_ref=value, dst_ref=values_landed.at[source],
            send_sem=value_send.at[step], recv_sem=value_recv.at[source],
            device_id={"tm": target}, device_id_type=MESH,
        )

    shifts = sorted(
        ((dy, dx, dc) for dy in range(groups // 8) for dx in range(4) for dc in range(2)),
        key=lambda m: -(min(m[0], groups // 8 - m[0]) + min(m[1], 4 - m[1])),
    )
    shifts.remove((0, 0, 0))

    def partner(step):
        dy, dx, dc = shifts[step - 1]
        y, x, core = lax.div(group, 8), lax.rem(lax.div(group, 2), 4), lax.rem(group, 2)
        return lax.rem(y + dy, groups // 8) * 8 + lax.rem(x + dx, 4) * 2 + lax.rem(core + dc, 2)

    def share(step, source, target):
        return pltpu.make_async_remote_copy(
            src_ref=summed, dst_ref=spread.at[source],
            send_sem=spread_send.at[step], recv_sem=spread_recv.at[source],
            device_id={"paths": target}, device_id_type=MESH,
        )

    for step in ORDER:
        line(step, me, lax.rem(me + step, SHARDS)).start()
    for step in ORDER:
        block(step, me, lax.rem(me + step, SHARDS)).start()
    landed[me] = part[me]
    values_landed[me] = value[...]
    end_sends(me, (0, 1, 2))
    by_source(EARLY, end_sends)
    by_source(LATE, end_sends)
    for source in everyone:

        @pl.when(me != source)
        def _():
            block(0, source, source).wait_recv()

    total = landed[0]
    for source in range(1, SHARDS):
        total = total + landed[source]
    summed[...] = total
    spread[group] = total
    for source in everyone:

        @pl.when(me != source)
        def _():
            line(0, source, source).wait_recv()

    for step in range(1, groups):
        share(step, group, partner(step)).start()
    for source in everyone:
        values[0:1, source * width : (source + 1) * width] = values_landed[source]
    for step in ORDER:
        block(step, me, lax.rem(me + step, SHARDS)).wait_send()
        line(step, me, lax.rem(me + step, SHARDS)).wait_send()
    for step in range(1, groups):
        share(step, group, partner(step)).wait_send()
    for step in range(1, groups):
        source = lax.rem(group + step, groups)
        share(0, source, source).wait_recv()
    total = spread[0]
    for source in range(1, groups):
        total = total + spread[source]
    vega[...] = total[:, 0:NF]


def local(
    start_curve, loadings, vols, shocks, exercise_bits, regress, date_slot,
    ck_rates, ck_numer, ck_survive,
):
    groups = lax.axis_size("paths")
    path_count = shocks.shape[2]
    width = path_count // SHARDS
    inside = pl.BlockSpec(memory_space=pltpu.VMEM)
    anywhere = pl.BlockSpec(memory_space=pl.ANY)
    small = pltpu.VMEM((PER, SHARDS, width), F32)
    lhs = pltpu.VMEM((NF, 256), BF16)
    plane = pltpu.VMEM((NF, width), F32)
    dates = pltpu.VMEM((PER, NF, width), F32)
    dma = pltpu.SemaphoreType.DMA
    vega, values = pl.pallas_call(
        functools.partial(kernel, NOTIONAL / (path_count * groups), groups),
        name="pathwise_vega",
        out_shape=[
            jax.ShapeDtypeStruct((PER, NF), F32),
            jax.ShapeDtypeStruct((1, path_count), F32),
        ],
        in_specs=[anywhere] * 10,
        out_specs=[inside] * 2,
        scratch_shapes=[
            pltpu.VMEM((1, NF), F32),
            pltpu.VMEM((4, NF), F32),
            pltpu.VMEM((SHARDS, PER, 4, width), F32),
            pltpu.VMEM((SHARDS, PER, width), jnp.int32),
            pltpu.VMEM((SHARDS, NF, width), F32),
            pltpu.VMEM((SHARDS, 1, width), F32),
            pltpu.VMEM((SHARDS, 1, width), F32),
            pltpu.VMEM((SHARDS, PER, NF), F32),
            pltpu.VMEM((SHARDS, PER, 6), F32),
            pltpu.VMEM((SHARDS, 1, PER), jnp.int32),
            pltpu.VMEM((128, 128), F32),
            pltpu.VMEM((256, 128), F32),
            lhs, lhs, lhs, lhs,
            pltpu.VMEM((SHARDS, PER, NF, 128), F32),
            pltpu.VMEM((PER * SHARDS, 128), F32),
            small, small, small, small,
            small, small, small,
            pltpu.VMEM((SHARDS, PER, 128), F32),
            pltpu.VMEM((SHARDS, PER, 128), F32),
            pltpu.VMEM((1, width), F32),
            pltpu.VMEM((SHARDS, 1, width), F32),
            pltpu.VMEM((PER, 128), F32),
            pltpu.VMEM((groups, PER, 128), F32),
        ]
        + [plane] * SHARDS
        + [plane] * SHARDS
        + [pltpu.VMEM((PER + 1, NF, width), F32)] * SHARDS
        + [dates] * SHARDS
        + [dates] * SHARDS
        + [pltpu.VMEM((PER, NF, 128), F32)] * SHARDS
        + [
            dma((KINDS, SHARDS)), dma((KINDS, SHARDS)), dma((KINDS + 2,)),
            dma((SHARDS,)), dma((SHARDS,)), dma((SHARDS,)), dma((SHARDS,)),
            dma((groups,)), dma((groups,)),
        ],
        compiler_params=pltpu.CompilerParams(
            collective_id=0, has_side_effects=True, vmem_limit_bytes=VMEM_LIMIT
        ),
    )(
        start_curve.reshape(1, NF), loadings, shocks, exercise_bits, ck_rates, ck_numer,
        ck_survive, vols, regress, date_slot.reshape(1, PER),
    )
    vega, values = pl.pallas_call(
        finish_kernel,
        name="finish",
        out_shape=[jax.ShapeDtypeStruct(x.shape, F32) for x in (vega, values)],
        in_specs=[inside] * 2,
        out_specs=[inside] * 2,
    )(vega, values)
    return (vega, values.reshape(path_count))


def finish_kernel(vega, values, vega_out, values_out):
    vega_out[...] = vega[...]
    values_out[...] = values[...]


def solution(mesh):
    return jax.shard_map(
        local,
        mesh=mesh,
        in_specs=(
            P(),
            P(),
            P("tm", None),
            P("tm", None, "paths"),
            P("tm", "paths"),
            P("tm", None),
            P("tm"),
            P("tm", None, "paths"),
            P("tm", "paths"),
            P("tm", "paths"),
        ),
        out_specs=(P("tm", None), P("paths")),
        check_vma=False,
    )
```
